128 devices in a mesh: seq: 128 (over x, y, z, core).
Axes of the slice: x: 4, y: 4, z: 4, core: 2. Of those that a mesh axis runs over, the one named last changes fastest.
Arguments:
- inputs: bfloat16 [131072, 768], P('seq'), may hold values from -6 to 6
- weight_one: bfloat16 [768, 3, 768], P('seq'), may hold values from -0.125 to 0.125
- weight_two: bfloat16 [768, 3, 768], P('seq'), may hold values from -0.125 to 0.125
- cotangent: bfloat16 [131072, 768], P('seq'), may hold values from -6 to 6
Outputs:
- outputs: bfloat16 [131072, 768], P('seq')
- input_grad: bfloat16 [131072, 768], P('seq')
- grad_one: float32 [768, 3, 768], P('seq')
- grad_two: float32 [768, 3, 768], P('seq')
The draws below stay inside these ranges and needn't reach their ends.
All inputs are finite; a program needn't handle non-finite values.
Results may differ from the reference program's by a relative error of at most 0.0056.
Values may be sent and summed in bfloat16 or wider, within the bound.
A program may use at most 128 MiB of HBM per device.

```python
import math
import jax
import jax.numpy as jnp
from jax import lax

C = 768
TAPS = 3
DILATION_A = 32
DILATION_B = 64
SEQ = 131072


def level_of(key, extent, split, least, high):
    level = 1.0
    for position, blocks in split:
        steps = jax.random.uniform(jax.random.fold_in(jax.random.fold_in(key, 6), position), (blocks,), jnp.float32, least / len(split), high / len(split))
        level = level * jnp.repeat(jnp.exp(steps), extent[position] // blocks).reshape((-1,) + (1,) * (len(extent) - 1 - position))
    return level


def centred(rng, shape, spread, limit, pieces=(), dtype=jnp.bfloat16):
    values = jax.random.normal(rng, shape, jnp.float32) * spread
    if len(pieces) > 0:
        values = level_of(rng, shape, pieces, -0.22, 0.18) * values
    return jnp.clip(values, min=-limit, max=limit).astype(dtype)


def setup_inputs(seed: int = 0) -> dict:
    arg_keys = jax.random.split(jax.random.key(seed), 5)
    return {
        "inputs": centred(arg_keys[0], (SEQ, C), 1.0, 6.0, ((0, 128),)),
        "weight_one": centred(arg_keys[1], (C, TAPS, C), (TAPS * C) ** -0.5, 0.125, ((0, 128),)),
        "weight_two": centred(arg_keys[2], (C, TAPS, C), (TAPS * C) ** -0.5, 0.125, ((0, 128),)),
        "cotangent": centred(arg_keys[3], (SEQ, C), 1.0, 6.0, ((0, 128),)),
    }


def normalize(layer_in):
    residual_in = layer_in.astype(jnp.float32)
    inv_rms = lax.rsqrt(lax.optimization_barrier(jnp.mean(residual_in * residual_in, axis=-1, keepdims=True)) + 1e-06)
    normed = residual_in * inv_rms
    active = (0.5 * normed * (1.0 + jax.scipy.special.erf(normed * 0.7071067811865476))).astype(jnp.bfloat16)
    return (residual_in, normed, inv_rms, active)

def slope_of(normed):
    return 0.5 * (1.0 + jax.scipy.special.erf(normed * 0.7071067811865476)) + normed * jnp.exp(-0.5 * normed * normed) * 0.3989422804014327

def forward_layer(layer_in, weight, spacing):
    residual_in, normed, inv_rms, active = normalize(layer_in)
    padded = jnp.pad(active, ((spacing, spacing), (0, 0)))
    length = layer_in.shape[0]
    mixed = jnp.zeros((length, weight.shape[2]), jnp.float32)
    for tap in range(3):
        mixed = mixed + jnp.dot(padded[tap * spacing:tap * spacing + length], weight[:, tap, :], preferred_element_type=jnp.float32)
    return ((residual_in + mixed).astype(jnp.bfloat16), padded, normed, inv_rms)

def backward_layer(grad_out, padded, normed, inv_rms, weight, spacing, grad_scale):
    length = grad_out.shape[0]
    terms = []
    for tap in range(3):
        terms.append(lax.dot_general(padded[tap * spacing:tap * spacing + length], grad_out, (((0,), (0,)), ((), ())), preferred_element_type=jnp.float32))
    weight_grad = jnp.stack(terms, axis=1) * grad_scale
    grad_pad = jnp.pad(grad_out, ((spacing, spacing), (0, 0)))
    act_grad = jnp.zeros((length, weight.shape[0]), jnp.float32)
    for tap in range(3):
        start_row = (2 - tap) * spacing
        act_grad = act_grad + lax.dot_general(grad_pad[start_row:start_row + length], weight[:, tap, :], (((1,), (1,)), ((), ())), preferred_element_type=jnp.float32)
    norm_grad = act_grad * slope_of(normed)
    passed = grad_out.astype(jnp.float32) + inv_rms * (norm_grad - normed * lax.optimization_barrier(jnp.mean(norm_grad * normed, axis=-1, keepdims=True)))
    return (passed.astype(jnp.bfloat16), weight_grad)

def reference(inputs, weight_one, weight_two, cotangent):
    grad_scale = 1.0 / math.sqrt(inputs.shape[0])
    hidden, pad_one, normed_one, inv_one = forward_layer(inputs, weight_one, DILATION_A)
    outputs, pad_two, normed_two, inv_two = forward_layer(hidden, weight_two, DILATION_B)
    hidden_grad, grad_two = backward_layer(cotangent, pad_two, normed_two, inv_two, weight_two, DILATION_B, grad_scale)
    input_grad, grad_one = backward_layer(hidden_grad, pad_one, normed_one, inv_one, weight_one, DILATION_A, grad_scale)
    return (outputs, input_grad, grad_one, grad_two)
```

```python
import math

import jax
import jax.numpy as jnp
from jax import lax
from jax.experimental import pallas as pl
from jax.experimental.pallas import tpu as pltpu
from jax.sharding import PartitionSpec as P

DILATION_A = 32
DILATION_B = 64
N = 128
C = 768
HALF = C // 2
L = 1024
BF = jnp.bfloat16
F32 = jnp.float32
MESH = pl.DeviceIdType.MESH
TM = 256


def body(
    scale,
    x_hbm, g_hbm, w_hbm,
    out_hbm, ig_hbm, gr_hbm,
    xb, a1p, h, a2p, g2p, g1p, at1, at2, W, s1, s2, ir1, ir2, G, stage, R0, A, H1, R1, B, S2R, T, S3S, S3R, ob, ib, gout,
    lsem, cs, cr, hs, hr, p1s, p1r, p2s, p2r, fs, fr, bs, br,
    x0s, x0r, x1s, x1r, x2s, x2r, x3s, x3r, x4s, x4r,
):
    me = lax.axis_index("seq")
    c = lax.rem(me, 2)
    z = lax.rem(me // 2, 4)
    y = lax.rem(me // 8, 4)
    x = me // 32
    g = me // 8

    def block(df, ds, o):
        xx = lax.rem(x + 4 + df * (1 - o) + ds * o, 4)
        yy = lax.rem(y + 4 + df * o + ds * (1 - o), 4)
        return 4 * xx + yy

    def dev(df, ds):
        return block(df, ds, c) * 8 + 2 * z + c

    sibling = me + 1 - 2 * c
    left = lax.rem(me + N - 1, N)
    right = lax.rem(me + 1, N)
    column = g * 8
    myf = x * (1 - c) + y * c
    mys = y * (1 - c) + x * c

    def remote(src, dst, send, recv, target):
        return pltpu.make_async_remote_copy(
            src_ref=src, dst_ref=dst, send_sem=send, recv_sem=recv, device_id=(target,), device_id_type=MESH
        )

    sent = []

    def send(*args):
        copy = remote(*args)
        copy.start()
        sent.append(copy)

    def arrived(dst, send_sem, recv_sem):
        remote(dst, dst, send_sem, recv_sem, sibling).wait_recv()

    load_x = pltpu.make_async_copy(x_hbm, xb, lsem.at[0])
    load_x.start()
    load_g = pltpu.make_async_copy(g_hbm, g2p.at[pl.ds(DILATION_B, L)], lsem.at[1])
    load_g.start()

    barrier = pltpu.get_barrier_semaphore()
    greet = []
    for k in range(1, 8):
        greet.append(column + lax.rem(me - column + k, 8))
    for k in range(1, 4):
        greet.append(dev(k, 0))
    greet += [dev(0, 1), dev(0, 3), left, right]
    for target in greet:
        pl.semaphore_signal(barrier, inc=1, device_id=(target,), device_id_type=MESH)
    pl.semaphore_wait(barrier, len(greet))

    cc = z // 2
    slot = 2 * lax.rem(z, 2) + c

    def column_send(l):
        for zt in range(4):
            target = column + 2 * zt + cc

            @pl.when(target != me)
            def _():
                remote(w_hbm.at[l], stage.at[l, :, slot], cs.at[l, zt], cr.at[l, slot], target).start()

            @pl.when(target == me)
            def _():
                pltpu.make_async_copy(w_hbm.at[l], stage.at[l, :, slot], cr.at[l, slot]).start()

    def column_wait(l):
        for j in range(4):
            source = column + 4 * c + j

            @pl.when(source != me)
            def _():
                arrived(stage.at[l, :, j], cs.at[l, 0], cr.at[l, j])

            @pl.when(source == me)
            def _():
                pltpu.make_async_copy(w_hbm.at[l], stage.at[l, :, j], cr.at[l, j]).wait()

    def column_sent(l):
        for zt in range(4):
            target = column + 2 * zt + cc

            @pl.when(target != me)
            def _():
                remote(w_hbm.at[l], stage.at[l, :, slot], cs.at[l, zt], cr.at[l, slot], target).wait_send()

    def blk(l, b, half):
        return W.at[l, :, b, half]

    def repack(l):
        row = lax.broadcasted_iota(jnp.int32, (24, 32), 0)
        col = lax.broadcasted_iota(jnp.int32, (24, 32), 1)
        pick = jnp.where(col == (row // 6) * 8 + lax.rem(row, 6), 1.0, 0.0).astype(BF)
        for k in range(3):
            dense = jnp.dot(pick, stage[l, k].reshape(32, C), preferred_element_type=F32)
            W[l, k, g, c] = dense.astype(BF)

    def ag_p1(l):
        for k in range(1, 4):
            send(blk(l, g, c), blk(l, g, c), p1s.at[l, k - 1], p1r.at[l, k - 1], dev(k, 0))

    def to_sibling(l, n, b):
        send(blk(l, b, c), blk(l, b, c), bs.at[l, n], br.at[l, n], sibling)

    def ag_p2(l, i):
        b = block(-i, 0, c)
        for d in range(2):
            send(blk(l, b, c), blk(l, b, c), p2s.at[l, d, i], p2r.at[l, d, i], dev(0, 1 + 2 * d))
        to_sibling(l, i, b)

    def ag_mid(l):
        for k in range(1, 4):
            arrived(blk(l, block(-k, 0, c), c), p1s.at[l, k - 1], p1r.at[l, k - 1])
            ag_p2(l, k)

    def ag_forward(l):
        for i in range(4):
            for d in range(2):
                b = block(-i, 3 - 2 * d, c)
                arrived(blk(l, b, c), p2s.at[l, d, i], p2r.at[l, d, i])
                part = W.at[l, :, b, c, :, pl.ds(HALF * d, HALF)]
                send(part, part, fs.at[l, d, i], fr.at[l, d, i], dev(0, 1 + 2 * d))
                to_sibling(l, 4 + 4 * d + i, b)

    def ag_last(l):
        for i in range(4):
            b = block(-i, 2, c)
            for d in range(2):
                part = W.at[l, :, b, c, :, pl.ds(HALF * d, HALF)]
                arrived(part, fs.at[l, d, i], fr.at[l, d, i])
            to_sibling(l, 12 + i, b)

    def ag_done(l):
        for n, ds in enumerate((0, 3, 1, 2)):
            for i in range(4):
                b = block(-i, ds, 1 - c)
                arrived(blk(l, b, 1 - c), bs.at[l, 4 * n + i], br.at[l, 4 * n + i])

    def halo_send(ref, d, n):
        send(ref.at[pl.ds(L, d)], ref.at[pl.ds(0, d)], hs.at[n, 0], hr.at[n, 0], right)
        send(ref.at[pl.ds(d, d)], ref.at[pl.ds(L + d, d)], hs.at[n, 1], hr.at[n, 1], left)

    def halo_wait(ref, d, n):
        arrived(ref.at[pl.ds(0, d)], hs.at[n, 0], hr.at[n, 0])
        arrived(ref.at[pl.ds(L + d, d)], hs.at[n, 1], hr.at[n, 1])

        @pl.when(me == 0)
        def _():
            ref[pl.ds(0, d), :] = jnp.zeros((d, C), BF)

        @pl.when(me == N - 1)
        def _():
            ref[pl.ds(L + d, d), :] = jnp.zeros((d, C), BF)

    def activate(xf, t0, ap, d, at, s_ref, ir_ref):
        inv = lax.rsqrt(jnp.mean(xf * xf, axis=-1, keepdims=True) + 1e-06)
        normed = xf * inv
        gate = 0.5 * (1.0 + lax.erf(normed * 0.7071067811865476))
        active = (normed * gate).astype(BF)
        ap[pl.ds(pl.multiple_of(t0 + d, 32), TM), :] = active
        at[:, pl.ds(t0, TM)] = active.T
        s_ref[pl.ds(t0, TM), :] = gate + normed * jnp.exp(-0.5 * normed * normed) * 0.3989422804014327
        ir_ref[pl.ds(t0, TM), :] = inv

    def tiles(fn, count=L // TM, size=TM):
        def step(i, carry):
            fn(pl.multiple_of(i * size, size))
            return carry

        lax.fori_loop(0, count, step, 0)

    def weight(l, k):
        return W[l, k].reshape(C, C)

    def forward(ap, d, l, t0):
        acc = jnp.zeros((TM, C), F32)
        for k in range(3):
            acc = acc + jnp.dot(
                ap[pl.ds(pl.multiple_of(t0 + k * d, 32), TM), :], weight(l, k), preferred_element_type=F32
            )
        return acc

    def backward(gp, d, l, x_ref, s_ref, ir_ref, t0):
        acc = jnp.zeros((TM, C), F32)
        for k in range(3):
            acc = acc + lax.dot_general(
                gp[pl.ds(pl.multiple_of(t0 + (2 - k) * d, 32), TM), :],
                weight(l, k),
                (((1,), (1,)), ((), ())),
                preferred_element_type=F32,
            )
        rows = pl.ds(t0, TM)
        inv = ir_ref[rows, :]
        normed = x_ref[rows, :].astype(F32) * inv
        norm_grad = acc * s_ref[rows, :]
        mean = jnp.mean(norm_grad * normed, axis=-1, keepdims=True)
        own = gp[pl.ds(pl.multiple_of(t0 + d, 32), TM), :].astype(F32)
        return (own + inv * (norm_grad - normed * mean)).astype(BF)

    def weight_grad(at, gp, d, l, k):
        rhs_start = (2 - k) * d

        def one(t0):
            acc = jnp.dot(at[pl.ds(t0, 384), :], gp[pl.ds(rhs_start, L), :], preferred_element_type=F32)
            b0 = t0 // 48
            G[l, k, pl.ds(b0, 8)] = acc.astype(BF).reshape(8, 2, 24, C)

        tiles(one, 2, 384)
        send(G.at[l, k, :, 1 - c], R0.at[l, k], x0s.at[l, k], x0r.at[l, k], sibling)

    def rs1(l, k):
        arrived(R0.at[l, k], x0s.at[l, k], x0r.at[l, k])

        def add(b, carry):
            s = b // 4
            f = lax.rem(b, 4)
            gb = f * (4 - 3 * c) + s * (1 + 3 * c)
            A[l, k, s, f] = (G[l, k, gb, c].astype(F32) + R0[l, k, gb].astype(F32)).astype(BF)
            return carry

        lax.fori_loop(0, 16, add, 0)
        far = lax.rem(mys + 2, 4)
        for d in range(2):
            send(
                A.at[l, k, far, :, :, pl.ds(HALF * d, HALF)], H1.at[l, k, d],
                x1s.at[l, k, d], x1r.at[l, k, d], dev(0, 1 + 2 * d),
            )

    def rs2(l, k):
        for d in range(2):
            arrived(H1.at[l, k, d], x1s.at[l, k, d], x1r.at[l, k, d])
            near = lax.rem(mys + 1 + 2 * d, 4)
            cols = pl.ds(HALF * d, HALF)
            A[l, k, near, :, :, cols] = (A[l, k, near, :, :, cols].astype(F32) + H1[l, k, d].astype(F32)).astype(BF)
            send(A.at[l, k, near], R1.at[l, k, d], x2s.at[l, k, d], x2r.at[l, k, d], dev(0, 1 + 2 * d))

    def rs3(l, k):
        for d in range(2):
            arrived(R1.at[l, k, d], x2s.at[l, k, d], x2r.at[l, k, d])
        B[l, k] = (A[l, k, mys].astype(F32) + R1[l, k, 0].astype(F32) + R1[l, k, 1].astype(F32)).astype(BF)
        for d in range(1, 4):
            send(
                B.at[l, k, lax.rem(myf + d, 4)], S2R.at[l, k, d - 1],
                x3s.at[l, k, d - 1], x3r.at[l, k, d - 1], dev(d, 0),
            )

    def rs4(l, k):
        for d in range(1, 4):
            arrived(S2R.at[l, k, d - 1], x3s.at[l, k, d - 1], x3r.at[l, k, d - 1])
        total = B[l, k, myf].astype(F32)
        for d in range(3):
            total = total + S2R[l, k, d].astype(F32)
        T[pl.ds(0, 24), :] = total
        T[pl.ds(24, 8), :] = jnp.zeros((8, C), F32)
        for j in range(4):
            S3S[l, j, k] = T[pl.ds(6 * j, 8), :].astype(BF)

    def rs5(l):
        for j in range(4):
            target = column + 4 * c + j

            @pl.when(target != me)
            def _():
                remote(S3S.at[l, j], S3R.at[l, z], x4s.at[l, j], x4r.at[l, z], target).start()

            @pl.when(target == me)
            def _():
                S3R[l, z] = S3S[l, j]

    def rs6(l):
        for zs in range(4):
            source = column + 2 * zs + cc

            @pl.when(source != me)
            def _():
                arrived(S3R.at[l, zs], x4s.at[l, 0], x4r.at[l, zs])

        total = S3R[l, 0].astype(F32)
        for zs in range(1, 4):
            total = total + S3R[l, zs].astype(F32)
        gout[l] = total * scale
        pltpu.make_async_copy(gout.at[l], gr_hbm.at[l], lsem.at[2 + l]).start()

    def rs_sent(l):
        for j in range(4):
            target = column + 4 * c + j

            @pl.when(target != me)
            def _():
                remote(S3S.at[l, j], S3R.at[l, z], x4s.at[l, j], x4r.at[l, z], target).wait_send()

    column_send(0)
    column_send(1)
    load_x.wait()
    tiles(lambda t0: activate(xb[pl.ds(t0, TM), :].astype(F32), t0, a1p, DILATION_A, at1, s1, ir1))
    column_wait(0)
    repack(0)
    ag_p1(0)
    ag_p2(0, 0)
    halo_send(a1p, DILATION_A, 0)
    ag_mid(0)
    column_wait(1)
    repack(1)
    ag_p1(1)
    load_g.wait()
    halo_send(g2p, DILATION_B, 2)
    ag_forward(0)
    ag_p2(1, 0)
    ag_mid(1)
    ag_last(0)
    halo_wait(a1p, DILATION_A, 0)
    ag_done(0)

    def first(t0):
        mixed = forward(a1p, DILATION_A, 0, t0)
        out = (xb[pl.ds(t0, TM), :].astype(F32) + mixed).astype(BF)
        h[pl.ds(t0, TM), :] = out
        activate(out.astype(F32), t0, a2p, DILATION_B, at2, s2, ir2)

    tiles(first)
    halo_send(a2p, DILATION_B, 1)
    ag_forward(1)
    halo_wait(g2p, DILATION_B, 2)
    weight_grad(at2, g2p, DILATION_B, 1, 0)
    ag_last(1)
    weight_grad(at2, g2p, DILATION_B, 1, 1)
    rs1(1, 0)
    weight_grad(at2, g2p, DILATION_B, 1, 2)
    rs1(1, 1)
    rs2(1, 0)
    ag_done(1)

    def second(t0):
        passed = backward(g2p, DILATION_B, 1, h, s2, ir2, t0)
        g1p[pl.ds(pl.multiple_of(t0 + DILATION_A, 32), TM), :] = passed

    tiles(second)
    halo_send(g1p, DILATION_A, 3)
    rs1(1, 2)
    rs2(1, 1)
    rs3(1, 0)
    weight_grad(at1, g1p, DILATION_A, 0, 1)
    halo_wait(g1p, DILATION_A, 3)
    rs2(1, 2)
    rs3(1, 1)
    rs4(1, 0)
    weight_grad(at1, g1p, DILATION_A, 0, 0)
    rs1(0, 1)
    rs3(1, 2)
    rs4(1, 1)
    weight_grad(at1, g1p, DILATION_A, 0, 2)
    rs1(0, 0)
    rs2(0, 1)
    rs4(1, 2)
    rs5(1)
    halo_wait(a2p, DILATION_B, 1)

    def last_forward(t0):
        mixed = forward(a2p, DILATION_B, 1, t0)
        rows = pl.ds(t0, TM)
        ob[rows, :] = (h[rows, :].astype(F32) + mixed).astype(BF)

    tiles(last_forward)
    store_out = pltpu.make_async_copy(ob, out_hbm, lsem.at[4])
    store_out.start()
    rs1(0, 2)
    rs2(0, 0)
    rs3(0, 1)
    rs6(1)

    def last_backward(t0):
        ib[pl.ds(t0, TM), :] = backward(g1p, DILATION_A, 0, xb, s1, ir1, t0)

    tiles(last_backward)
    store_in = pltpu.make_async_copy(ib, ig_hbm, lsem.at[5])
    store_in.start()
    rs2(0, 2)
    rs3(0, 0)
    rs4(0, 1)
    rs3(0, 2)
    rs4(0, 0)
    rs4(0, 2)
    rs5(0)
    rs6(0)

    for copy in sent:
        copy.wait_send()
    for l in range(2):
        column_sent(l)
        rs_sent(l)
        pltpu.make_async_copy(gout.at[l], gr_hbm.at[l], lsem.at[2 + l]).wait()
    store_out.wait()
    store_in.wait()


def per_device(inputs, weight_one, weight_two, cotangent):
    scale = 1.0 / math.sqrt(inputs.shape[0] * lax.axis_size("seq"))
    shards = jnp.stack([weight_one, weight_two]).transpose(0, 2, 1, 3)
    shards = jnp.pad(shards, ((0, 0), (0, 0), (0, 2), (0, 0)))
    anywhere = pl.BlockSpec(memory_space=pl.ANY)
    vmem = pltpu.VMEM
    dma = pltpu.SemaphoreType.DMA

    def kernel(*refs):
        body(scale, *refs)

    outputs, input_grad, grads = pl.pallas_call(
        kernel,
        out_shape=(
            jax.ShapeDtypeStruct((L, C), BF),
            jax.ShapeDtypeStruct((L, C), BF),
            jax.ShapeDtypeStruct((2, 3, 8, C), F32),
        ),
        in_specs=[anywhere] * 3,
        out_specs=(anywhere,) * 3,
        scratch_shapes=[
            vmem((L, C), BF),
            vmem((L + 2 * DILATION_A, C), BF),
            vmem((L, C), BF),
            vmem((L + 2 * DILATION_B, C), BF),
            vmem((L + 2 * DILATION_B, C), BF),
            vmem((L + 2 * DILATION_A, C), BF),
            vmem((C, L), BF),
            vmem((C, L), BF),
            vmem((2, 3, 16, 2, 24, C), BF),
            vmem((L, C), F32),
            vmem((L, C), F32),
            vmem((L, 1), F32),
            vmem((L, 1), F32),
            vmem((2, 3, 16, 2, 24, C), BF),
            vmem((2, 3, 4, 8, C), BF),
            vmem((2, 3, 16, 24, C), BF),
            vmem((2, 3, 4, 4, 24, C), BF),
            vmem((2, 3, 2, 4, 24, HALF), BF),
            vmem((2, 3, 2, 4, 24, C), BF),
            vmem((2, 3, 4, 24, C), BF),
            vmem((2, 3, 3, 24, C), BF),
            vmem((32, C), F32),
            vmem((2, 4, 3, 8, C), BF),
            vmem((2, 4, 3, 8, C), BF),
            vmem((L, C), BF),
            vmem((L, C), BF),
            vmem((2, 3, 8, C), F32),
            dma((6,)),
            dma((2, 4)), dma((2, 4)),
            dma((4, 2)), dma((4, 2)),
            dma((2, 3)), dma((2, 3)),
            dma((2, 2, 4)), dma((2, 2, 4)),
            dma((2, 2, 4)), dma((2, 2, 4)),
            dma((2, 16)), dma((2, 16)),
            dma((2, 3)), dma((2, 3)),
            dma((2, 3, 2)), dma((2, 3, 2)),
            dma((2, 3, 2)), dma((2, 3, 2)),
            dma((2, 3, 3)), dma((2, 3, 3)),
            dma((2, 4)), dma((2, 4)),
        ],
        compiler_params=pltpu.CompilerParams(
            collective_id=0, has_side_effects=True, vmem_limit_bytes=64000000
        ),
    )(inputs, cotangent, shards)
    grads = grads[:, :, :6, :].transpose(0, 2, 1, 3)
    return (outputs, input_grad, grads[0], grads[1])


def solution(mesh):
    in_specs = (P("seq", None), P("seq", None, None), P("seq", None, None), P("seq", None))
    out_specs = (P("seq", None), P("seq", None), P("seq", None, None), P("seq", None, None))
    return jax.shard_map(
        per_device, mesh=mesh, in_specs=in_specs, out_specs=out_specs, check_vma=False
    )
```

```python
import math

import jax
import jax.numpy as jnp
from jax import lax
from jax.experimental import pallas as pl
from jax.experimental.pallas import tpu as pltpu
from jax.sharding import PartitionSpec as P

DILATION_A = 32
DILATION_B = 64
N = 128
C = 768
HALF = C // 2
L = 1024
BF = jnp.bfloat16
F32 = jnp.float32
MESH = pl.DeviceIdType.MESH
TM = 256


def body(
    scale,
    x_hbm, g_hbm, w_hbm,
    out_hbm, ig_hbm, gr_hbm,
    xb, a1p, h, a2p, g2p, g1p, at1, at2, W, s1, s2, ir1, ir2, G, stage, R0, A, H1, R1, B, S2R, T, S3S, S3R, gout,
    lsem, cs, cr, hs, hr, p1s, p1r, p2s, p2r, fs, fr, bs, br,
    x0s, x0r, x1s, x1r, x2s, x2r, x3s, x3r, x4s, x4r,
):
    me = lax.axis_index("seq")
    c = lax.rem(me, 2)
    z = lax.rem(me // 2, 4)
    y = lax.rem(me // 8, 4)
    x = me // 32

    def place(df, ds, o):
        dx, dy = (df, ds) if o == 0 else (ds, df)
        return lax.rem(x + dx, 4), lax.rem(y + dy, 4)

    def dev(df, ds, o):
        xx, yy = place(df, ds, o)
        return (4 * xx + yy) * 8 + 2 * z + c

    firsts = (x, y)
    seconds = (y, x)
    sibling = me + 1 - 2 * c
    left = lax.rem(me + N - 1, N)
    right = lax.rem(me + 1, N)
    column = (4 * x + y) * 8

    def remote(src, dst, send, recv, target):
        return pltpu.make_async_remote_copy(
            src_ref=src, dst_ref=dst, send_sem=send, recv_sem=recv, device_id=(target,), device_id_type=MESH
        )

    sent = []

    def send(*args):
        copy = remote(*args)
        copy.start()
        sent.append(copy)

    def arrived(dst, send_sem, recv_sem):
        remote(dst, dst, send_sem, recv_sem, sibling).wait_recv()

    load_x = pltpu.make_async_copy(x_hbm, xb, lsem.at[0])
    load_x.start()
    load_g = pltpu.make_async_copy(g_hbm, g2p.at[pl.ds(DILATION_B, L)], lsem.at[1])
    load_g.start()

    barrier = pltpu.get_barrier_semaphore()
    greet = [column + lax.rem(me - column + k, 8) for k in range(1, 8)]
    for o in range(2):
        greet += [dev(k, 0, o) for k in range(1, 4)]
    greet += [left, right]
    for target in greet:
        pl.semaphore_signal(barrier, inc=1, device_id=(target,), device_id_type=MESH)

    cc = z // 2
    slot = 2 * lax.rem(z, 2) + c

    def column_send(l):
        for zt in range(4):
            target = column + 2 * zt + cc

            @pl.when(target != me)
            def _():
                remote(w_hbm.at[l], stage.at[l, :, slot], cs.at[l, zt], cr.at[l, slot], target).start()

            @pl.when(target == me)
            def _():
                pltpu.make_async_copy(w_hbm.at[l], stage.at[l, :, slot], cr.at[l, slot]).start()

    def column_wait(l):
        for j in range(4):
            source = column + 4 * c + j

            @pl.when(source != me)
            def _():
                arrived(stage.at[l, :, j], cs.at[l, 0], cr.at[l, j])

            @pl.when(source == me)
            def _():
                pltpu.make_async_copy(w_hbm.at[l], stage.at[l, :, j], cr.at[l, j]).wait()

    def column_sent(l):
        for zt in range(4):
            target = column + 2 * zt + cc

            @pl.when(target != me)
            def _():
                remote(w_hbm.at[l], stage.at[l, :, slot], cs.at[l, zt], cr.at[l, slot], target).wait_send()

    def repack(l):
        row = lax.broadcasted_iota(jnp.int32, (24, 32), 0)
        col = lax.broadcasted_iota(jnp.int32, (24, 32), 1)
        pick = jnp.where(col == (row // 6) * 8 + lax.rem(row, 6), 1.0, 0.0).astype(BF)
        for k in range(3):
            dense = jnp.dot(pick, stage[l, k].reshape(32, C), preferred_element_type=F32)
            W[l, k, x, y, c] = dense.astype(BF)

    OFFSET = (0, 3, 1, 2)

    def share(k, o, d):
        width = 128 if (k + o + d) % 2 == 0 else 256
        return HALF * o + (0 if d == 0 else HALF - width), width

    def grp(l, k, o, n, half, start=None, width=HALF):
        cols = pl.ds(HALF * o if start is None else start, width)
        s = lax.rem(seconds[o] + OFFSET[n], 4)
        if o == 0:
            return W.at[l, k, :, s, half, :, cols]
        return W.at[l, k, s, :, half, :, cols]

    def ag_p1(l, k):
        for o in range(2):
            for d in range(1, 4):
                ref = W.at[l, k, x, y, c, :, pl.ds(HALF * o, HALF)]
                send(ref, ref, p1s.at[l, k, o, d - 1], p1r.at[l, k, o, d - 1], dev(d, 0, o))

    def to_sibling(l, k, o, n):
        ref = grp(l, k, o, n, c)
        send(ref, ref, bs.at[l, k, o, n], br.at[l, k, o, n], sibling)

    def ag_p2(l, k):
        for o in range(2):
            for d in range(1, 4):
                xx, yy = place(4 - d, 0, o)
                arrived(W.at[l, k, xx, yy, c, :, pl.ds(HALF * o, HALF)], p1s.at[l, k, o, d - 1], p1r.at[l, k, o, d - 1])
            for d in range(2):
                ref = grp(l, k, o, 0, c)
                send(ref, ref, p2s.at[l, k, o, d], p2r.at[l, k, o, d], dev(0, 1 + 2 * d, o))
            to_sibling(l, k, o, 0)

    def ag_f(l, k):
        for o in range(2):
            for d in range(2):
                arrived(grp(l, k, o, 1 + d, c), p2s.at[l, k, o, d], p2r.at[l, k, o, d])
                part = grp(l, k, o, 1 + d, c, *share(k, o, d))
                send(part, part, fs.at[l, k, o, d], fr.at[l, k, o, d], dev(0, 1 + 2 * d, o))
                to_sibling(l, k, o, 1 + d)

    def ag_e(l, k):
        for o in range(2):
            for d in range(2):
                arrived(grp(l, k, o, 3, c, *share(k, o, d)), fs.at[l, k, o, d], fr.at[l, k, o, d])
            to_sibling(l, k, o, 3)

    def ag_done(l, k):
        for o in range(2):
            for n in range(4):
                arrived(grp(l, k, o, n, 1 - c), bs.at[l, k, o, n], br.at[l, k, o, n])

    def halo_copies(ref, d, n):
        return (
            remote(ref.at[pl.ds(L, d)], ref.at[pl.ds(0, d)], hs.at[n, 0], hr.at[n, 0], right),
            remote(ref.at[pl.ds(d, d)], ref.at[pl.ds(L + d, d)], hs.at[n, 1], hr.at[n, 1], left),
        )

    def halo_send(ref, d, n):
        for copy in halo_copies(ref, d, n):
            copy.start()

    def halo_sent(ref, d, n):
        for copy in halo_copies(ref, d, n):
            copy.wait_send()

    def halo_wait(ref, d, n):
        arrived(ref.at[pl.ds(0, d)], hs.at[n, 0], hr.at[n, 0])
        arrived(ref.at[pl.ds(L + d, d)], hs.at[n, 1], hr.at[n, 1])

        @pl.when(me == 0)
        def _():
            ref[pl.ds(0, d), :] = jnp.zeros((d, C), BF)

        @pl.when(me == N - 1)
        def _():
            ref[pl.ds(L + d, d), :] = jnp.zeros((d, C), BF)

    def activate(xf, t0, ap, d, at, s_ref, ir_ref):
        inv = lax.rsqrt(jnp.mean(xf * xf, axis=-1, keepdims=True) + 1e-06)
        normed = xf * inv
        gate = 0.5 * (1.0 + lax.erf(normed * 0.7071067811865476))
        active = (normed * gate).astype(BF)
        ap[pl.ds(pl.multiple_of(t0 + d, 32), TM), :] = active
        at[:, pl.ds(t0, TM)] = active.T
        s_ref[pl.ds(t0, TM), :] = gate + normed * jnp.exp(-0.5 * normed * normed) * 0.3989422804014327
        ir_ref[pl.ds(t0, TM), :] = inv

    def tiles(fn, count, size=TM, low=0):
        def step(i, carry):
            fn(pl.multiple_of(i * size, size))
            return carry

        lax.fori_loop(low, count, step, 0)

    def tile(fn, i):
        tiles(fn, i + 1, TM, i)

    def weight(l, k):
        return W[l, k].reshape(C, C)

    def term(ap, d, l, k, t0):
        return jnp.dot(ap[pl.ds(pl.multiple_of(t0 + k * d, 32), TM), :], weight(l, k), preferred_element_type=F32)

    def forward(ap, d, l, t0):
        acc = jnp.zeros((TM, C), F32)
        for k in range(3):
            acc = acc + term(ap, d, l, k, t0)
        return acc

    def backward(gp, d, l, x_ref, s_ref, ir_ref, t0):
        acc = jnp.zeros((TM, C), F32)
        for k in range(3):
            acc = acc + lax.dot_general(
                gp[pl.ds(pl.multiple_of(t0 + (2 - k) * d, 32), TM), :],
                weight(l, k),
                (((1,), (1,)), ((), ())),
                preferred_element_type=F32,
            )
        rows = pl.ds(t0, TM)
        inv = ir_ref[rows, :]
        normed = x_ref[rows, :].astype(F32) * inv
        norm_grad = acc * s_ref[rows, :]
        mean = jnp.mean(norm_grad * normed, axis=-1, keepdims=True)
        own = gp[pl.ds(pl.multiple_of(t0 + d, 32), TM), :].astype(F32)
        return (own + inv * (norm_grad - normed * mean)).astype(BF)

    def weight_grad(at, gp, d, l, k):
        rhs_start = (2 - k) * d

        def one(t0):
            acc = jnp.dot(at[pl.ds(t0, 384), :], gp[pl.ds(rhs_start, L), :], preferred_element_type=F32)
            G[l, k, pl.ds(t0 // 48, 8)] = acc.astype(BF).reshape(8, 2, 24, C)

        tiles(one, 2, 384)
        send(G.at[l, k, :, 1 - c], R0.at[l, k], x0s.at[l, k], x0r.at[l, k], sibling)

    def act_one(t0):
        activate(xb[pl.ds(t0, TM), :].astype(F32), t0, a1p, DILATION_A, at1, s1, ir1)

    def first_a(t0):
        s2[pl.ds(t0, TM), :] = term(a1p, DILATION_A, 0, 1, t0)

    def first_b(t0):
        s2[pl.ds(t0, TM), :] += term(a1p, DILATION_A, 0, 0, t0)

    def first(t0):
        mixed = s2[pl.ds(t0, TM), :] + term(a1p, DILATION_A, 0, 2, t0)
        out = (xb[pl.ds(t0, TM), :].astype(F32) + mixed).astype(BF)
        h[pl.ds(t0, TM), :] = out
        activate(out.astype(F32), t0, a2p, DILATION_B, at2, s2, ir2)

    def second(t0):
        passed = backward(g2p, DILATION_B, 1, h, s2, ir2, t0)
        g1p[pl.ds(pl.multiple_of(t0 + DILATION_A, 32), TM), :] = passed

    def last_forward(t0):
        mixed = forward(a2p, DILATION_B, 1, t0)
        rows = pl.ds(t0, TM)
        g2p[rows, :] = (h[rows, :].astype(F32) + mixed).astype(BF)

    def last_backward(t0):
        a2p[pl.ds(t0, TM), :] = backward(g1p, DILATION_A, 0, xb, s1, ir1, t0)

    store_out = pltpu.make_async_copy(g2p.at[pl.ds(0, L)], out_hbm, lsem.at[4])
    store_in = pltpu.make_async_copy(a2p.at[pl.ds(0, L)], ig_hbm, lsem.at[5])

    def rs1(l, k):
        arrived(R0.at[l, k], x0s.at[l, k], x0r.at[l, k])

        def add(b, carry):
            hi = b // 4
            lo = lax.rem(b, 4)
            total = G[l, k, b, c] + R0[l, k, b]
            A[l, k, 0, lo, hi] = total[:, :HALF]
            A[l, k, 1, hi, lo] = total[:, HALF:]
            return carry

        lax.fori_loop(0, 16, add, 0)
        for o in range(2):
            far = lax.rem(seconds[o] + 2, 4)
            for d in range(2):
                start, width = share(k, o, d)
                cols = pl.ds(start - HALF * o, width)
                send(
                    A.at[l, k, o, far, :, :, cols], H1.at[l, k, o, :, :, cols],
                    x1s.at[l, k, o, d], x1r.at[l, k, o, d], dev(0, 1 + 2 * d, o),
                )

    def rs2(l, k):
        for o in range(2):
            for d in range(2):
                start, width = share(k, o, d)
                cols = pl.ds(start - HALF * o, width)
                arrived(H1.at[l, k, o, :, :, cols], x1s.at[l, k, o, d], x1r.at[l, k, o, d])
                near = lax.rem(seconds[o] + 1 + 2 * d, 4)
                A[l, k, o, near, :, :, cols] = A[l, k, o, near, :, :, cols] + H1[l, k, o, :, :, cols]
                send(
                    A.at[l, k, o, near], R1.at[l, k, o, d],
                    x2s.at[l, k, o, d], x2r.at[l, k, o, d], dev(0, 1 + 2 * d, o),
                )

    def rs3(l, k):
        for o in range(2):
            for d in range(2):
                arrived(R1.at[l, k, o, d], x2s.at[l, k, o, d], x2r.at[l, k, o, d])
            B[l, k, o] = (
                A[l, k, o, seconds[o]].astype(F32) + R1[l, k, o, 0].astype(F32) + R1[l, k, o, 1].astype(F32)
            ).astype(BF)
            for d in range(1, 4):
                send(
                    B.at[l, k, o, lax.rem(firsts[o] + d, 4)], S2R.at[l, k, o, d - 1],
                    x3s.at[l, k, o, d - 1], x3r.at[l, k, o, d - 1], dev(d, 0, o),
                )

    def rs4(l, k):
        for o in range(2):
            for d in range(1, 4):
                arrived(S2R.at[l, k, o, d - 1], x3s.at[l, k, o, d - 1], x3r.at[l, k, o, d - 1])
            total = B[l, k, o, firsts[o]].astype(F32)
            for d in range(3):
                total = total + S2R[l, k, o, d].astype(F32)
            T[pl.ds(0, 24), pl.ds(HALF * o, HALF)] = total
        T[pl.ds(24, 8), :] = jnp.zeros((8, C), F32)
        for j in range(4):
            S3S[l, j, k] = T[pl.ds(6 * j, 8), :].astype(BF)

    def rs5(l):
        for j in range(4):
            target = column + 4 * c + j

            @pl.when(target != me)
            def _():
                remote(S3S.at[l, j], S3R.at[l, z], x4s.at[l, j], x4r.at[l, z], target).start()

            @pl.when(target == me)
            def _():
                S3R[l, z] = S3S[l, j]

    def rs6(l):
        for zs in range(4):
            source = column + 2 * zs + cc

            @pl.when(source != me)
            def _():
                arrived(S3R.at[l, zs], x4s.at[l, 0], x4r.at[l, zs])

        total = S3R[l, 0].astype(F32)
        for zs in range(1, 4):
            total = total + S3R[l, zs].astype(F32)
        gout[l] = total * scale
        pltpu.make_async_copy(gout.at[l], gr_hbm.at[l], lsem.at[2 + l]).start()

    def rs_sent(l):
        for j in range(4):
            target = column + 4 * c + j

            @pl.when(target != me)
            def _():
                remote(S3S.at[l, j], S3R.at[l, z], x4s.at[l, j], x4r.at[l, z], target).wait_send()

    load_x.wait()
    tiles(act_one, 2)
    pl.semaphore_wait(barrier, len(greet))
    column_send(0)
    column_send(1)
    tiles(act_one, 4, TM, 2)
    column_wait(0)
    repack(0)
    ag_p1(0, 1)
    ag_p1(0, 0)
    ag_p1(0, 2)
    halo_send(a1p, DILATION_A, 0)
    column_wait(1)
    repack(1)
    ag_p2(0, 1)
    ag_p2(0, 0)
    ag_p2(0, 2)
    load_g.wait()
    ag_f(0, 1)
    ag_p1(1, 1)
    ag_p1(1, 0)
    ag_p1(1, 2)
    ag_f(0, 0)
    halo_send(g2p, DILATION_B, 2)
    halo_wait(a1p, DILATION_A, 0)
    ag_e(0, 1)
    ag_f(0, 2)
    ag_p2(1, 1)
    ag_done(0, 1)
    tiles(first_a, 4)
    ag_e(0, 0)
    ag_p2(1, 0)
    ag_p2(1, 2)
    ag_e(0, 2)
    ag_done(0, 0)
    tiles(first_b, 4)
    ag_done(0, 2)
    ag_f(1, 1)
    tiles(first, 2)
    ag_f(1, 0)
    ag_e(1, 1)
    tiles(first, 4, TM, 2)
    ag_f(1, 2)
    ag_e(1, 0)
    halo_send(a2p, DILATION_B, 1)
    halo_wait(g2p, DILATION_B, 2)
    weight_grad(at2, g2p, DILATION_B, 1, 1)
    weight_grad(at2, g2p, DILATION_B, 1, 2)
    ag_e(1, 2)
    rs1(1, 1)
    weight_grad(at2, g2p, DILATION_B, 1, 0)
    rs1(1, 2)
    for k in range(3):
        ag_done(1, k)
    tile(second, 0)
    rs2(1, 1)
    tile(second, 1)
    rs1(1, 0)
    rs2(1, 2)
    tile(second, 2)
    rs3(1, 1)
    tile(second, 3)
    halo_send(g1p, DILATION_A, 3)
    rs2(1, 0)
    rs3(1, 2)
    weight_grad(at1, g1p, DILATION_A, 0, 1)
    rs4(1, 1)
    halo_wait(g1p, DILATION_A, 3)
    weight_grad(at1, g1p, DILATION_A, 0, 2)
    rs1(0, 1)
    rs3(1, 0)
    weight_grad(at1, g1p, DILATION_A, 0, 0)
    rs1(0, 2)
    rs4(1, 2)
    halo_wait(a2p, DILATION_B, 1)
    halo_sent(g2p, DILATION_B, 2)
    tile(last_forward, 0)
    rs1(0, 0)
    rs2(0, 1)
    tile(last_forward, 1)
    rs4(1, 0)
    rs5(1)
    rs2(0, 2)
    tile(last_forward, 2)
    rs2(0, 0)
    rs3(0, 1)
    tile(last_forward, 3)
    store_out.start()
    rs3(0, 2)
    rs6(1)
    halo_sent(a2p, DILATION_B, 1)
    tile(last_backward, 0)
    rs3(0, 0)
    rs4(0, 1)
    tile(last_backward, 1)
    rs4(0, 2)
    tile(last_backward, 2)
    rs4(0, 0)
    rs5(0)
    tile(last_backward, 3)
    store_in.start()
    rs6(0)

    for copy in sent:
        copy.wait_send()
    halo_sent(a1p, DILATION_A, 0)
    halo_sent(g1p, DILATION_A, 3)
    for l in range(2):
        column_sent(l)
        rs_sent(l)
        pltpu.make_async_copy(gout.at[l], gr_hbm.at[l], lsem.at[2 + l]).wait()
    store_out.wait()
    store_in.wait()


def per_device(inputs, weight_one, weight_two, cotangent):
    scale = 1.0 / math.sqrt(inputs.shape[0] * lax.axis_size("seq"))
    shards = jnp.stack([weight_one, weight_two]).transpose(0, 2, 1, 3)
    shards = jnp.pad(shards, ((0, 0), (0, 0), (0, 2), (0, 0)))
    anywhere = pl.BlockSpec(memory_space=pl.ANY)
    vmem = pltpu.VMEM
    dma = pltpu.SemaphoreType.DMA

    def kernel(*refs):
        body(scale, *refs)

    outputs, input_grad, grads = pl.pallas_call(
        kernel,
        out_shape=(
            jax.ShapeDtypeStruct((L, C), BF),
            jax.ShapeDtypeStruct((L, C), BF),
            jax.ShapeDtypeStruct((2, 3, 8, C), F32),
        ),
        in_specs=[anywhere] * 3,
        out_specs=(anywhere,) * 3,
        scratch_shapes=[
            vmem((L, C), BF),
            vmem((L + 2 * DILATION_A, C), BF),
            vmem((L, C), BF),
            vmem((L + 2 * DILATION_B, C), BF),
            vmem((L + 2 * DILATION_B, C), BF),
            vmem((L + 2 * DILATION_A, C), BF),
            vmem((C, L), BF),
            vmem((C, L), BF),
            vmem((2, 3, 4, 4, 2, 24, C), BF),
            vmem((L, C), F32),
            vmem((L, C), F32),
            vmem((L, 1), F32),
            vmem((L, 1), F32),
            vmem((2, 3, 16, 2, 24, C), BF),
            vmem((2, 3, 4, 8, C), BF),
            vmem((2, 3, 16, 24, C), BF),
            vmem((2, 3, 2, 4, 4, 24, HALF), BF),
            vmem((2, 3, 2, 4, 24, HALF), BF),
            vmem((2, 3, 2, 2, 4, 24, HALF), BF),
            vmem((2, 3, 2, 4, 24, HALF), BF),
            vmem((2, 3, 2, 3, 24, HALF), BF),
            vmem((32, C), F32),
            vmem((2, 4, 3, 8, C), BF),
            vmem((2, 4, 3, 8, C), BF),
            vmem((2, 3, 8, C), F32),
            dma((6,)),
            dma((2, 4)), dma((2, 4)),
            dma((4, 2)), dma((4, 2)),
            dma((2, 3, 2, 3)), dma((2, 3, 2, 3)),
            dma((2, 3, 2, 2)), dma((2, 3, 2, 2)),
            dma((2, 3, 2, 2)), dma((2, 3, 2, 2)),
            dma((2, 3, 2, 4)), dma((2, 3, 2, 4)),
            dma((2, 3)), dma((2, 3)),
            dma((2, 3, 2, 2)), dma((2, 3, 2, 2)),
            dma((2, 3, 2, 2)), dma((2, 3, 2, 2)),
            dma((2, 3, 2, 3)), dma((2, 3, 2, 3)),
            dma((2, 4)), dma((2, 4)),
        ],
        compiler_params=pltpu.CompilerParams(
            collective_id=0, has_side_effects=True, vmem_limit_bytes=50500000
        ),
    )(inputs, cotangent, shards)
    grads = grads[:, :, :6, :].transpose(0, 2, 1, 3)
    return (outputs, input_grad, grads[0], grads[1])


def solution(mesh):
    in_specs = (P("seq", None), P("seq", None, None), P("seq", None, None), P("seq", None))
    out_specs = (P("seq", None), P("seq", None), P("seq", None, None), P("seq", None, None))
    return jax.shard_map(
        per_device, mesh=mesh, in_specs=in_specs, out_specs=out_specs, check_vma=False
    )
```

```python
import math

import jax
import jax.numpy as jnp
from jax import lax
from jax.experimental import pallas as pl
from jax.experimental.pallas import tpu as pltpu
from jax.sharding import PartitionSpec as P

DILATION_A = 32
DILATION_B = 64
N = 128
C = 768
HALF = C // 2
L = 1024
BF = jnp.bfloat16
F32 = jnp.float32
MESH = pl.DeviceIdType.MESH
TM = 256


def body(
    scale,
    x_hbm, g_hbm, w_hbm,
    out_hbm, ig_hbm, gr_hbm,
    xb, a1p, h, a2p, g2p, g1p, at1, at2, W, s1, s2, ir1, ir2, G, stage, R0, A, H1, R1, B, S2R, T, S3S, S3R, gout,
    lsem, cs, cr, hs, hr, p1s, p1r, p2s, p2r, fs, fr, bs, br,
    x0s, x0r, x1s, x1r, x2s, x2r, x3s, x3r, x4s, x4r,
):
    me = lax.axis_index("seq")
    c = lax.rem(me, 2)
    z = lax.rem(me // 2, 4)
    y = lax.rem(me // 8, 4)
    x = me // 32

    def place(df, ds, o):
        dx, dy = (df, ds) if o == 0 else (ds, df)
        return lax.rem(x + dx, 4), lax.rem(y + dy, 4)

    def dev(df, ds, o):
        xx, yy = place(df, ds, o)
        return (4 * xx + yy) * 8 + 2 * z + c

    firsts = (x, y)
    seconds = (y, x)
    sibling = me + 1 - 2 * c
    left = lax.rem(me + N - 1, N)
    right = lax.rem(me + 1, N)
    column = (4 * x + y) * 8

    def remote(src, dst, send, recv, target):
        return pltpu.make_async_remote_copy(
            src_ref=src, dst_ref=dst, send_sem=send, recv_sem=recv, device_id=(target,), device_id_type=MESH
        )

    sent = []

    def send(*args):
        copy = remote(*args)
        copy.start()
        sent.append(copy)

    def arrived(dst, send_sem, recv_sem):
        remote(dst, dst, send_sem, recv_sem, sibling).wait_recv()

    load_x = pltpu.make_async_copy(x_hbm, xb, lsem.at[0])
    load_x.start()
    load_g = pltpu.make_async_copy(g_hbm, g2p.at[pl.ds(DILATION_B, L)], lsem.at[1])
    load_g.start()

    barrier = pltpu.get_barrier_semaphore()
    greet = [column + lax.rem(me - column + k, 8) for k in range(1, 8)]
    for o in range(2):
        greet += [dev(k, 0, o) for k in range(1, 4)]
    greet += [left, right]
    for target in greet:
        pl.semaphore_signal(barrier, inc=1, device_id=(target,), device_id_type=MESH)

    cc = z // 2
    slot = 2 * lax.rem(z, 2) + c

    def column_send(l):
        for zt in range(4):
            target = column + 2 * zt + cc

            @pl.when(target != me)
            def _():
                remote(w_hbm.at[l], stage.at[l, :, slot], cs.at[l, zt], cr.at[l, slot], target).start()

            @pl.when(target == me)
            def _():
                pltpu.make_async_copy(w_hbm.at[l], stage.at[l, :, slot], cr.at[l, slot]).start()

    def column_wait(l):
        for j in range(4):
            source = column + 4 * c + j

            @pl.when(source != me)
            def _():
                arrived(stage.at[l, :, j], cs.at[l, 0], cr.at[l, j])

            @pl.when(source == me)
            def _():
                pltpu.make_async_copy(w_hbm.at[l], stage.at[l, :, j], cr.at[l, j]).wait()

    def column_sent(l):
        for zt in range(4):
            target = column + 2 * zt + cc

            @pl.when(target != me)
            def _():
                remote(w_hbm.at[l], stage.at[l, :, slot], cs.at[l, zt], cr.at[l, slot], target).wait_send()

    def repack(l):
        row = lax.broadcasted_iota(jnp.int32, (24, 32), 0)
        col = lax.broadcasted_iota(jnp.int32, (24, 32), 1)
        pick = jnp.where(col == (row // 6) * 8 + lax.rem(row, 6), 1.0, 0.0).astype(BF)
        for k in range(3):
            dense = jnp.dot(pick, stage[l, k].reshape(32, C), preferred_element_type=F32)
            W[l, k, x, y, c] = dense.astype(BF)

    OFFSET = (0, 3, 1, 2)

    def share(k, o, d):
        width = 128 if (k + o + d) % 2 == 0 else 256
        return HALF * o + (0 if d == 0 else HALF - width), width

    def grp(l, k, o, n, half, start=None, width=HALF):
        cols = pl.ds(HALF * o if start is None else start, width)
        s = lax.rem(seconds[o] + OFFSET[n], 4)
        if o == 0:
            return W.at[l, k, :, s, half, :, cols]
        return W.at[l, k, s, :, half, :, cols]

    def ag_p1(l, k):
        for o in range(2):
            for d in range(1, 4):
                ref = W.at[l, k, x, y, c, :, pl.ds(HALF * o, HALF)]
                send(ref, ref, p1s.at[l, k, o, d - 1], p1r.at[l, k, o, d - 1], dev(d, 0, o))

    def to_sibling(l, k, o, n):
        ref = grp(l, k, o, n, c)
        send(ref, ref, bs.at[l, k, o, n], br.at[l, k, o, n], sibling)

    def ag_p2(l, k):
        for o in range(2):
            for d in range(1, 4):
                xx, yy = place(4 - d, 0, o)
                arrived(W.at[l, k, xx, yy, c, :, pl.ds(HALF * o, HALF)], p1s.at[l, k, o, d - 1], p1r.at[l, k, o, d - 1])
            for d in range(2):
                ref = grp(l, k, o, 0, c)
                send(ref, ref, p2s.at[l, k, o, d], p2r.at[l, k, o, d], dev(0, 1 + 2 * d, o))
            to_sibling(l, k, o, 0)

    def ag_f(l, k):
        for o in range(2):
            for d in range(2):
                arrived(grp(l, k, o, 1 + d, c), p2s.at[l, k, o, d], p2r.at[l, k, o, d])
                part = grp(l, k, o, 1 + d, c, *share(k, o, d))
                send(part, part, fs.at[l, k, o, d], fr.at[l, k, o, d], dev(0, 1 + 2 * d, o))
                to_sibling(l, k, o, 1 + d)

    def ag_e(l, k):
        for o in range(2):
            for d in range(2):
                arrived(grp(l, k, o, 3, c, *share(k, o, d)), fs.at[l, k, o, d], fr.at[l, k, o, d])
            to_sibling(l, k, o, 3)

    def ag_done(l, k):
        for o in range(2):
            for n in range(4):
                arrived(grp(l, k, o, n, 1 - c), bs.at[l, k, o, n], br.at[l, k, o, n])

    def halo_copies(ref, d, n):
        return (
            remote(ref.at[pl.ds(L, d)], ref.at[pl.ds(0, d)], hs.at[n, 0], hr.at[n, 0], right),
            remote(ref.at[pl.ds(d, d)], ref.at[pl.ds(L + d, d)], hs.at[n, 1], hr.at[n, 1], left),
        )

    def halo_send(ref, d, n):
        for copy in halo_copies(ref, d, n):
            copy.start()

    def halo_sent(ref, d, n):
        for copy in halo_copies(ref, d, n):
            copy.wait_send()

    def halo_wait(ref, d, n):
        arrived(ref.at[pl.ds(0, d)], hs.at[n, 0], hr.at[n, 0])
        arrived(ref.at[pl.ds(L + d, d)], hs.at[n, 1], hr.at[n, 1])

        @pl.when(me == 0)
        def _():
            ref[pl.ds(0, d), :] = jnp.zeros((d, C), BF)

        @pl.when(me == N - 1)
        def _():
            ref[pl.ds(L + d, d), :] = jnp.zeros((d, C), BF)

    def activate(xf, t0, ap, d, at, s_ref, ir_ref):
        inv = lax.rsqrt(jnp.mean(xf * xf, axis=-1, keepdims=True) + 1e-06)
        normed = xf * inv
        gate = 0.5 * (1.0 + lax.erf(normed * 0.7071067811865476))
        active = (normed * gate).astype(BF)
        ap[pl.ds(pl.multiple_of(t0 + d, 32), TM), :] = active
        at[:, pl.ds(t0, TM)] = active.T
        s_ref[pl.ds(t0, TM), :] = gate + normed * jnp.exp(-0.5 * normed * normed) * 0.3989422804014327
        ir_ref[pl.ds(t0, TM), :] = inv

    def tiles(fn, count, size=TM, low=0):
        def step(i, carry):
            fn(pl.multiple_of(i * size, size))
            return carry

        lax.fori_loop(low, count, step, 0)

    def tile(fn, i):
        tiles(fn, i + 1, TM, i)

    def weight(l, k):
        return W[l, k].reshape(C, C)

    def term(ap, d, l, k, t0):
        return jnp.dot(ap[pl.ds(pl.multiple_of(t0 + k * d, 32), TM), :], weight(l, k), preferred_element_type=F32)

    def forward(ap, d, l, t0):
        acc = jnp.zeros((TM, C), F32)
        for k in range(3):
            acc = acc + term(ap, d, l, k, t0)
        return acc

    def backward(gp, d, l, x_ref, s_ref, ir_ref, t0):
        acc = jnp.zeros((TM, C), F32)
        for k in range(3):
            acc = acc + lax.dot_general(
                gp[pl.ds(pl.multiple_of(t0 + (2 - k) * d, 32), TM), :],
                weight(l, k),
                (((1,), (1,)), ((), ())),
                preferred_element_type=F32,
            )
        rows = pl.ds(t0, TM)
        inv = ir_ref[rows, :]
        normed = x_ref[rows, :].astype(F32) * inv
        norm_grad = acc * s_ref[rows, :]
        mean = jnp.mean(norm_grad * normed, axis=-1, keepdims=True)
        own = gp[pl.ds(pl.multiple_of(t0 + d, 32), TM), :].astype(F32)
        return (own + inv * (norm_grad - normed * mean)).astype(BF)

    def weight_grad(at, gp, d, l, k):
        rhs_start = (2 - k) * d

        def one(t0):
            acc = jnp.dot(at[pl.ds(t0, 384), :], gp[pl.ds(rhs_start, L), :], preferred_element_type=F32)
            G[l, k, pl.ds(t0 // 48, 8)] = acc.astype(BF).reshape(8, 2, 24, C)

        tiles(one, 2, 384)
        send(G.at[l, k, :, 1 - c], R0.at[l, k], x0s.at[l, k], x0r.at[l, k], sibling)

    def act_one(t0):
        activate(xb[pl.ds(t0, TM), :].astype(F32), t0, a1p, DILATION_A, at1, s1, ir1)

    def first_a(t0):
        s2[pl.ds(t0, TM), :] = term(a1p, DILATION_A, 0, 1, t0)

    def first_b(t0):
        s2[pl.ds(t0, TM), :] += term(a1p, DILATION_A, 0, 0, t0)

    def first(t0):
        mixed = s2[pl.ds(t0, TM), :] + term(a1p, DILATION_A, 0, 2, t0)
        out = (xb[pl.ds(t0, TM), :].astype(F32) + mixed).astype(BF)
        h[pl.ds(t0, TM), :] = out
        activate(out.astype(F32), t0, a2p, DILATION_B, at2, s2, ir2)

    def second(t0):
        passed = backward(g2p, DILATION_B, 1, h, s2, ir2, t0)
        g1p[pl.ds(pl.multiple_of(t0 + DILATION_A, 32), TM), :] = passed

    def last_forward(t0):
        mixed = forward(a2p, DILATION_B, 1, t0)
        rows = pl.ds(t0, TM)
        g2p[rows, :] = (h[rows, :].astype(F32) + mixed).astype(BF)

    def last_backward(t0):
        a2p[pl.ds(t0, TM), :] = backward(g1p, DILATION_A, 0, xb, s1, ir1, t0)

    store_out = pltpu.make_async_copy(g2p.at[pl.ds(0, L)], out_hbm, lsem.at[4])
    store_in = pltpu.make_async_copy(a2p.at[pl.ds(0, L)], ig_hbm, lsem.at[5])

    def rs1(l, k):
        arrived(R0.at[l, k], x0s.at[l, k], x0r.at[l, k])

        def add(b, carry):
            hi = b // 4
            lo = lax.rem(b, 4)
            total = G[l, k, b, c] + R0[l, k, b]
            A[l, k, 0, lo, hi] = total[:, :HALF]
            A[l, k, 1, hi, lo] = total[:, HALF:]
            return carry

        lax.fori_loop(0, 16, add, 0)
        for o in range(2):
            far = lax.rem(seconds[o] + 2, 4)
            for d in range(2):
                start, width = share(k, o, d)
                cols = pl.ds(start - HALF * o, width)
                send(
                    A.at[l, k, o, far, :, :, cols], H1.at[l, k, o, :, :, cols],
                    x1s.at[l, k, o, d], x1r.at[l, k, o, d], dev(0, 1 + 2 * d, o),
                )

    def rs2(l, k):
        for o in range(2):
            for d in range(2):
                start, width = share(k, o, d)
                cols = pl.ds(start - HALF * o, width)
                arrived(H1.at[l, k, o, :, :, cols], x1s.at[l, k, o, d], x1r.at[l, k, o, d])
                near = lax.rem(seconds[o] + 1 + 2 * d, 4)
                A[l, k, o, near, :, :, cols] = A[l, k, o, near, :, :, cols] + H1[l, k, o, :, :, cols]
                send(
                    A.at[l, k, o, near], R1.at[l, k, o, d],
                    x2s.at[l, k, o, d], x2r.at[l, k, o, d], dev(0, 1 + 2 * d, o),
                )

    def rs3(l, k):
        for o in range(2):
            for d in range(2):
                arrived(R1.at[l, k, o, d], x2s.at[l, k, o, d], x2r.at[l, k, o, d])
            B[l, k, o] = (
                A[l, k, o, seconds[o]].astype(F32) + R1[l, k, o, 0].astype(F32) + R1[l, k, o, 1].astype(F32)
            ).astype(BF)
            for d in range(1, 4):
                send(
                    B.at[l, k, o, lax.rem(firsts[o] + d, 4)], S2R.at[l, k, o, d - 1],
                    x3s.at[l, k, o, d - 1], x3r.at[l, k, o, d - 1], dev(d, 0, o),
                )

    def rs4(l, k):
        for o in range(2):
            for d in range(1, 4):
                arrived(S2R.at[l, k, o, d - 1], x3s.at[l, k, o, d - 1], x3r.at[l, k, o, d - 1])
            total = B[l, k, o, firsts[o]].astype(F32)
            for d in range(3):
                total = total + S2R[l, k, o, d].astype(F32)
            T[pl.ds(0, 24), pl.ds(HALF * o, HALF)] = total
        T[pl.ds(24, 8), :] = jnp.zeros((8, C), F32)
        for j in range(4):
            S3S[l, j, k] = T[pl.ds(6 * j, 8), :].astype(BF)

    def rs5(l):
        for j in range(4):
            target = column + 4 * c + j

            @pl.when(target != me)
            def _():
                remote(S3S.at[l, j], S3R.at[l, z], x4s.at[l, j], x4r.at[l, z], target).start()

            @pl.when(target == me)
            def _():
                S3R[l, z] = S3S[l, j]

    def rs6(l):
        for zs in range(4):
            source = column + 2 * zs + cc

            @pl.when(source != me)
            def _():
                arrived(S3R.at[l, zs], x4s.at[l, 0], x4r.at[l, zs])

        total = S3R[l, 0].astype(F32)
        for zs in range(1, 4):
            total = total + S3R[l, zs].astype(F32)
        gout[l] = total * scale
        pltpu.make_async_copy(gout.at[l], gr_hbm.at[l], lsem.at[2 + l]).start()

    def rs_sent(l):
        for j in range(4):
            target = column + 4 * c + j

            @pl.when(target != me)
            def _():
                remote(S3S.at[l, j], S3R.at[l, z], x4s.at[l, j], x4r.at[l, z], target).wait_send()

    load_x.wait()
    tiles(act_one, 2)
    pl.semaphore_wait(barrier, len(greet))
    column_send(0)
    column_send(1)
    tiles(act_one, 4, TM, 2)
    column_wait(0)
    repack(0)
    ag_p1(0, 1)
    ag_p1(0, 0)
    ag_p1(0, 2)
    halo_send(a1p, DILATION_A, 0)
    column_wait(1)
    repack(1)
    ag_p2(0, 1)
    ag_p2(0, 0)
    ag_p2(0, 2)
    load_g.wait()
    ag_f(0, 1)
    ag_p1(1, 1)
    ag_p1(1, 0)
    ag_p1(1, 2)
    ag_f(0, 0)
    halo_send(g2p, DILATION_B, 2)
    halo_wait(a1p, DILATION_A, 0)
    ag_e(0, 1)
    ag_f(0, 2)
    ag_p2(1, 1)
    ag_done(0, 1)
    tiles(first_a, 4)
    ag_e(0, 0)
    ag_p2(1, 0)
    ag_p2(1, 2)
    ag_e(0, 2)
    ag_done(0, 0)
    tiles(first_b, 4)
    ag_done(0, 2)
    ag_f(1, 1)
    tiles(first, 2)
    ag_f(1, 0)
    ag_e(1, 1)
    tiles(first, 4, TM, 2)
    ag_f(1, 2)
    ag_e(1, 0)
    halo_send(a2p, DILATION_B, 1)
    halo_wait(g2p, DILATION_B, 2)
    weight_grad(at2, g2p, DILATION_B, 1, 1)
    weight_grad(at2, g2p, DILATION_B, 1, 2)
    ag_e(1, 2)
    rs1(1, 1)
    weight_grad(at2, g2p, DILATION_B, 1, 0)
    rs1(1, 2)
    for k in range(3):
        ag_done(1, k)
    tile(second, 0)
    rs2(1, 1)
    tile(second, 3)
    halo_send(g1p, DILATION_A, 3)
    rs1(1, 0)
    rs2(1, 2)
    tile(second, 1)
    rs3(1, 1)
    tile(second, 2)
    rs2(1, 0)
    rs3(1, 2)
    weight_grad(at1, g1p, DILATION_A, 0, 1)
    rs4(1, 1)
    halo_wait(g1p, DILATION_A, 3)
    weight_grad(at1, g1p, DILATION_A, 0, 2)
    rs1(0, 1)
    rs3(1, 0)
    weight_grad(at1, g1p, DILATION_A, 0, 0)
    rs1(0, 2)
    rs4(1, 2)
    halo_wait(a2p, DILATION_B, 1)
    halo_sent(g2p, DILATION_B, 2)
    tile(last_forward, 0)
    rs1(0, 0)
    rs2(0, 1)
    tile(last_forward, 1)
    rs4(1, 0)
    rs5(1)
    rs2(0, 2)
    tile(last_forward, 2)
    rs2(0, 0)
    rs3(0, 1)
    tile(last_forward, 3)
    store_out.start()
    rs3(0, 2)
    rs6(1)
    halo_sent(a2p, DILATION_B, 1)
    tile(last_backward, 0)
    rs3(0, 0)
    rs4(0, 1)
    tile(last_backward, 1)
    rs4(0, 2)
    tile(last_backward, 2)
    rs4(0, 0)
    rs5(0)
    tile(last_backward, 3)
    store_in.start()
    rs6(0)

    for copy in sent:
        copy.wait_send()
    halo_sent(a1p, DILATION_A, 0)
    halo_sent(g1p, DILATION_A, 3)
    for l in range(2):
        column_sent(l)
        rs_sent(l)
        pltpu.make_async_copy(gout.at[l], gr_hbm.at[l], lsem.at[2 + l]).wait()
    store_out.wait()
    store_in.wait()


def per_device(inputs, weight_one, weight_two, cotangent):
    scale = 1.0 / math.sqrt(inputs.shape[0] * lax.axis_size("seq"))
    shards = jnp.stack([weight_one, weight_two]).transpose(0, 2, 1, 3)
    shards = jnp.pad(shards, ((0, 0), (0, 0), (0, 2), (0, 0)))
    anywhere = pl.BlockSpec(memory_space=pl.ANY)
    vmem = pltpu.VMEM
    dma = pltpu.SemaphoreType.DMA

    def kernel(*refs):
        body(scale, *refs)

    outputs, input_grad, grads = pl.pallas_call(
        kernel,
        out_shape=(
            jax.ShapeDtypeStruct((L, C), BF),
            jax.ShapeDtypeStruct((L, C), BF),
            jax.ShapeDtypeStruct((2, 3, 8, C), F32),
        ),
        in_specs=[anywhere] * 3,
        out_specs=(anywhere,) * 3,
        scratch_shapes=[
            vmem((L, C), BF),
            vmem((L + 2 * DILATION_A, C), BF),
            vmem((L, C), BF),
            vmem((L + 2 * DILATION_B, C), BF),
            vmem((L + 2 * DILATION_B, C), BF),
            vmem((L + 2 * DILATION_A, C), BF),
            vmem((C, L), BF),
            vmem((C, L), BF),
            vmem((2, 3, 4, 4, 2, 24, C), BF),
            vmem((L, C), F32),
            vmem((L, C), F32),
            vmem((L, 1), F32),
            vmem((L, 1), F32),
            vmem((2, 3, 16, 2, 24, C), BF),
            vmem((2, 3, 4, 8, C), BF),
            vmem((2, 3, 16, 24, C), BF),
            vmem((2, 3, 2, 4, 4, 24, HALF), BF),
            vmem((2, 3, 2, 4, 24, HALF), BF),
            vmem((2, 3, 2, 2, 4, 24, HALF), BF),
            vmem((2, 3, 2, 4, 24, HALF), BF),
            vmem((2, 3, 2, 3, 24, HALF), BF),
            vmem((32, C), F32),
            vmem((2, 4, 3, 8, C), BF),
            vmem((2, 4, 3, 8, C), BF),
            vmem((2, 3, 8, C), F32),
            dma((6,)),
            dma((2, 4)), dma((2, 4)),
            dma((4, 2)), dma((4, 2)),
            dma((2, 3, 2, 3)), dma((2, 3, 2, 3)),
            dma((2, 3, 2, 2)), dma((2, 3, 2, 2)),
            dma((2, 3, 2, 2)), dma((2, 3, 2, 2)),
            dma((2, 3, 2, 4)), dma((2, 3, 2, 4)),
            dma((2, 3)), dma((2, 3)),
            dma((2, 3, 2, 2)), dma((2, 3, 2, 2)),
            dma((2, 3, 2, 2)), dma((2, 3, 2, 2)),
            dma((2, 3, 2, 3)), dma((2, 3, 2, 3)),
            dma((2, 4)), dma((2, 4)),
        ],
        compiler_params=pltpu.CompilerParams(
            collective_id=0, has_side_effects=True, vmem_limit_bytes=50500000
        ),
    )(inputs, cotangent, shards)
    grads = grads[:, :, :6, :].transpose(0, 2, 1, 3)
    return (outputs, input_grad, grads[0], grads[1])


def solution(mesh):
    in_specs = (P("seq", None), P("seq", None, None), P("seq", None, None), P("seq", None))
    out_specs = (P("seq", None), P("seq", None), P("seq", None, None), P("seq", None, None))
    return jax.shard_map(
        per_device, mesh=mesh, in_specs=in_specs, out_specs=out_specs, check_vma=False
    )
```

```python
import math

import jax
import jax.numpy as jnp
from jax import lax
from jax.experimental import pallas as pl
from jax.experimental.pallas import tpu as pltpu
from jax.sharding import PartitionSpec as P

DILATION_A = 32
DILATION_B = 64
N = 128
C = 768
HALF = C // 2
L = 1024
BF = jnp.bfloat16
F32 = jnp.float32
MESH = pl.DeviceIdType.MESH
TM = 256


def body(
    scale,
    x_hbm, g_hbm, w_hbm,
    out_hbm, ig_hbm, gr_hbm,
    xb, a1p, h, a2p, g2p, g1p, at1, at2, W, s1, s2, ir1, ir2, G, stage, R0, A, H1, R1, B, S2R, T, S3S, S3R, gout,
    lsem, cs, cr, hs, hr, p1s, p1r, p2s, p2r, fs, fr, bs, br,
    x0s, x0r, x1s, x1r, x2s, x2r, x3s, x3r, x4s, x4r,
):
    me = lax.axis_index("seq")
    c = lax.rem(me, 2)
    z = lax.rem(me // 2, 4)
    y = lax.rem(me // 8, 4)
    x = me // 32

    def place(df, ds, o):
        dx, dy = (df, ds) if o == 0 else (ds, df)
        return lax.rem(x + dx, 4), lax.rem(y + dy, 4)

    def dev(df, ds, o):
        xx, yy = place(df, ds, o)
        return (4 * xx + yy) * 8 + 2 * z + c

    firsts = (x, y)
    seconds = (y, x)
    sibling = me + 1 - 2 * c
    left = lax.rem(me + N - 1, N)
    right = lax.rem(me + 1, N)
    column = (4 * x + y) * 8

    def remote(src, dst, send, recv, target):
        return pltpu.make_async_remote_copy(
            src_ref=src, dst_ref=dst, send_sem=send, recv_sem=recv, device_id=(target,), device_id_type=MESH
        )

    sent = []

    def send(*args):
        copy = remote(*args)
        copy.start()
        sent.append(copy)

    def arrived(dst, send_sem, recv_sem):
        remote(dst, dst, send_sem, recv_sem, sibling).wait_recv()

    load_x = pltpu.make_async_copy(x_hbm, xb, lsem.at[0])
    load_x.start()
    load_g = pltpu.make_async_copy(g_hbm, g2p.at[pl.ds(DILATION_B, L)], lsem.at[1])
    load_g.start()

    barrier = pltpu.get_barrier_semaphore()
    greet = [column + lax.rem(me - column + k, 8) for k in range(1, 8)]
    for o in range(2):
        greet += [dev(k, 0, o) for k in range(1, 4)]
    greet += [left, right]
    for target in greet:
        pl.semaphore_signal(barrier, inc=1, device_id=(target,), device_id_type=MESH)

    cc = z // 2
    slot = 2 * lax.rem(z, 2) + c

    def column_send(l):
        for zt in range(4):
            target = column + 2 * zt + cc

            @pl.when(target != me)
            def _():
                remote(w_hbm.at[l], stage.at[l, :, slot], cs.at[l, zt], cr.at[l, slot], target).start()

            @pl.when(target == me)
            def _():
                pltpu.make_async_copy(w_hbm.at[l], stage.at[l, :, slot], cr.at[l, slot]).start()

    def column_wait(l):
        for j in range(4):
            source = column + 4 * c + j

            @pl.when(source != me)
            def _():
                arrived(stage.at[l, :, j], cs.at[l, 0], cr.at[l, j])

            @pl.when(source == me)
            def _():
                pltpu.make_async_copy(w_hbm.at[l], stage.at[l, :, j], cr.at[l, j]).wait()

    def column_sent(l):
        for zt in range(4):
            target = column + 2 * zt + cc

            @pl.when(target != me)
            def _():
                remote(w_hbm.at[l], stage.at[l, :, slot], cs.at[l, zt], cr.at[l, slot], target).wait_send()

    def repack(l):
        row = lax.broadcasted_iota(jnp.int32, (24, 32), 0)
        col = lax.broadcasted_iota(jnp.int32, (24, 32), 1)
        pick = jnp.where(col == (row // 6) * 8 + lax.rem(row, 6), 1.0, 0.0).astype(BF)
        for k in range(3):
            dense = jnp.dot(pick, stage[l, k].reshape(32, C), preferred_element_type=F32)
            W[l, k, x, y, c] = dense.astype(BF)

    OFFSET = (0, 3, 1, 2)

    def share(k, o, d):
        width = 128 if (k + o + d) % 2 == 0 else 256
        return HALF * o + (0 if d == 0 else HALF - width), width

    def grp(l, k, o, n, half, start=None, width=HALF):
        cols = pl.ds(HALF * o if start is None else start, width)
        s = lax.rem(seconds[o] + OFFSET[n], 4)
        if o == 0:
            return W.at[l, k, :, s, half, :, cols]
        return W.at[l, k, s, :, half, :, cols]

    def ag_p1(l, k):
        for o in range(2):
            for d in range(1, 4):
                ref = W.at[l, k, x, y, c, :, pl.ds(HALF * o, HALF)]
                send(ref, ref, p1s.at[l, k, o, d - 1], p1r.at[l, k, o, d - 1], dev(d, 0, o))

    def to_sibling(l, k, o, n):
        ref = grp(l, k, o, n, c)
        send(ref, ref, bs.at[l, k, o, n], br.at[l, k, o, n], sibling)

    def ag_p2(l, k):
        for o in range(2):
            for d in range(1, 4):
                xx, yy = place(4 - d, 0, o)
                arrived(W.at[l, k, xx, yy, c, :, pl.ds(HALF * o, HALF)], p1s.at[l, k, o, d - 1], p1r.at[l, k, o, d - 1])
            for d in range(2):
                ref = grp(l, k, o, 0, c)
                send(ref, ref, p2s.at[l, k, o, d], p2r.at[l, k, o, d], dev(0, 1 + 2 * d, o))
            to_sibling(l, k, o, 0)

    def ag_f(l, k):
        for o in range(2):
            for d in range(2):
                arrived(grp(l, k, o, 1 + d, c), p2s.at[l, k, o, d], p2r.at[l, k, o, d])
                part = grp(l, k, o, 1 + d, c, *share(k, o, d))
                send(part, part, fs.at[l, k, o, d], fr.at[l, k, o, d], dev(0, 1 + 2 * d, o))
                to_sibling(l, k, o, 1 + d)

    def ag_e(l, k):
        for o in range(2):
            for d in range(2):
                arrived(grp(l, k, o, 3, c, *share(k, o, d)), fs.at[l, k, o, d], fr.at[l, k, o, d])
            to_sibling(l, k, o, 3)

    def ag_done(l, k):
        for o in range(2):
            for n in range(4):
                arrived(grp(l, k, o, n, 1 - c), bs.at[l, k, o, n], br.at[l, k, o, n])

    def halo_copies(ref, d, n):
        return (
            remote(ref.at[pl.ds(L, d)], ref.at[pl.ds(0, d)], hs.at[n, 0], hr.at[n, 0], right),
            remote(ref.at[pl.ds(d, d)], ref.at[pl.ds(L + d, d)], hs.at[n, 1], hr.at[n, 1], left),
        )

    def halo_send(ref, d, n):
        for copy in halo_copies(ref, d, n):
            copy.start()

    def halo_sent(ref, d, n):
        for copy in halo_copies(ref, d, n):
            copy.wait_send()

    def halo_wait(ref, d, n):
        arrived(ref.at[pl.ds(0, d)], hs.at[n, 0], hr.at[n, 0])
        arrived(ref.at[pl.ds(L + d, d)], hs.at[n, 1], hr.at[n, 1])

        @pl.when(me == 0)
        def _():
            ref[pl.ds(0, d), :] = jnp.zeros((d, C), BF)

        @pl.when(me == N - 1)
        def _():
            ref[pl.ds(L + d, d), :] = jnp.zeros((d, C), BF)

    def activate(xf, t0, ap, d, at, s_ref, ir_ref):
        inv = lax.rsqrt(jnp.mean(xf * xf, axis=-1, keepdims=True) + 1e-06)
        normed = xf * inv
        gate = 0.5 * (1.0 + lax.erf(normed * 0.7071067811865476))
        active = (normed * gate).astype(BF)
        ap[pl.ds(pl.multiple_of(t0 + d, 32), TM), :] = active
        at[:, pl.ds(t0, TM)] = active.T
        s_ref[pl.ds(t0, TM), :] = gate + normed * jnp.exp(-0.5 * normed * normed) * 0.3989422804014327
        ir_ref[pl.ds(t0, TM), :] = inv

    def tiles(fn, count, size=TM, low=0):
        def step(i, carry):
            fn(pl.multiple_of(i * size, size))
            return carry

        lax.fori_loop(low, count, step, 0)

    def tile(fn, i):
        tiles(fn, i + 1, TM, i)

    def weight(l, k):
        return W[l, k].reshape(C, C)

    def term(ap, d, l, k, t0):
        return jnp.dot(ap[pl.ds(pl.multiple_of(t0 + k * d, 32), TM), :], weight(l, k), preferred_element_type=F32)

    def forward(ap, d, l, t0):
        acc = jnp.zeros((TM, C), F32)
        for k in range(3):
            acc = acc + term(ap, d, l, k, t0)
        return acc

    def backward(gp, d, l, x_ref, s_ref, ir_ref, t0):
        acc = jnp.zeros((TM, C), F32)
        for k in range(3):
            acc = acc + lax.dot_general(
                gp[pl.ds(pl.multiple_of(t0 + (2 - k) * d, 32), TM), :],
                weight(l, k),
                (((1,), (1,)), ((), ())),
                preferred_element_type=F32,
            )
        rows = pl.ds(t0, TM)
        inv = ir_ref[rows, :]
        normed = x_ref[rows, :].astype(F32) * inv
        norm_grad = acc * s_ref[rows, :]
        mean = jnp.mean(norm_grad * normed, axis=-1, keepdims=True)
        own = gp[pl.ds(pl.multiple_of(t0 + d, 32), TM), :].astype(F32)
        return (own + inv * (norm_grad - normed * mean)).astype(BF)

    def weight_grad(at, gp, d, l, k):
        rhs_start = (2 - k) * d

        def one(t0):
            acc = jnp.dot(at[pl.ds(t0, 384), :], gp[pl.ds(rhs_start, L), :], preferred_element_type=F32)
            G[l, k, pl.ds(t0 // 48, 8)] = acc.astype(BF).reshape(8, 2, 24, C)

        tiles(one, 2, 384)
        send(G.at[l, k, :, 1 - c], R0.at[l, k], x0s.at[l, k], x0r.at[l, k], sibling)

    def act_one(t0):
        activate(xb[pl.ds(t0, TM), :].astype(F32), t0, a1p, DILATION_A, at1, s1, ir1)

    def first_a(t0):
        s2[pl.ds(t0, TM), :] = term(a1p, DILATION_A, 0, 1, t0)

    def first_b(t0):
        s2[pl.ds(t0, TM), :] += term(a1p, DILATION_A, 0, 0, t0)

    def first(t0):
        mixed = s2[pl.ds(t0, TM), :] + term(a1p, DILATION_A, 0, 2, t0)
        out = (xb[pl.ds(t0, TM), :].astype(F32) + mixed).astype(BF)
        h[pl.ds(t0, TM), :] = out
        activate(out.astype(F32), t0, a2p, DILATION_B, at2, s2, ir2)

    def second(t0):
        passed = backward(g2p, DILATION_B, 1, h, s2, ir2, t0)
        g1p[pl.ds(pl.multiple_of(t0 + DILATION_A, 32), TM), :] = passed

    def last_forward(t0):
        mixed = forward(a2p, DILATION_B, 1, t0)
        rows = pl.ds(t0, TM)
        g2p[rows, :] = (h[rows, :].astype(F32) + mixed).astype(BF)

    def last_backward(t0):
        a2p[pl.ds(t0, TM), :] = backward(g1p, DILATION_A, 0, xb, s1, ir1, t0)

    store_out = pltpu.make_async_copy(g2p.at[pl.ds(0, L)], out_hbm, lsem.at[4])
    store_in = pltpu.make_async_copy(a2p.at[pl.ds(0, L)], ig_hbm, lsem.at[5])

    def rs1(l, k):
        arrived(R0.at[l, k], x0s.at[l, k], x0r.at[l, k])

        def add(hi, carry):
            for lo in range(4):
                total = G[l, k, 4 * hi + lo, c] + R0[l, k, 4 * hi + lo]
                A[l, k, 0, lo, hi] = total[:, :HALF]
                A[l, k, 1, hi, lo] = total[:, HALF:]
            return carry

        lax.fori_loop(0, 4, add, 0)
        for o in range(2):
            far = lax.rem(seconds[o] + 2, 4)
            for d in range(2):
                start, width = share(k, o, d)
                cols = pl.ds(start - HALF * o, width)
                send(
                    A.at[l, k, o, far, :, :, cols], H1.at[l, k, o, :, :, cols],
                    x1s.at[l, k, o, d], x1r.at[l, k, o, d], dev(0, 1 + 2 * d, o),
                )

    def rs2(l, k):
        for o in range(2):
            for d in range(2):
                start, width = share(k, o, d)
                cols = pl.ds(start - HALF * o, width)
                arrived(H1.at[l, k, o, :, :, cols], x1s.at[l, k, o, d], x1r.at[l, k, o, d])
                near = lax.rem(seconds[o] + 1 + 2 * d, 4)
                A[l, k, o, near, :, :, cols] = A[l, k, o, near, :, :, cols] + H1[l, k, o, :, :, cols]
                send(
                    A.at[l, k, o, near], R1.at[l, k, o, d],
                    x2s.at[l, k, o, d], x2r.at[l, k, o, d], dev(0, 1 + 2 * d, o),
                )

    def rs3(l, k):
        for o in range(2):
            for d in range(2):
                arrived(R1.at[l, k, o, d], x2s.at[l, k, o, d], x2r.at[l, k, o, d])
            B[l, k, o] = (
                A[l, k, o, seconds[o]].astype(F32) + R1[l, k, o, 0].astype(F32) + R1[l, k, o, 1].astype(F32)
            ).astype(BF)
            for d in range(1, 4):
                send(
                    B.at[l, k, o, lax.rem(firsts[o] + d, 4)], S2R.at[l, k, o, d - 1],
                    x3s.at[l, k, o, d - 1], x3r.at[l, k, o, d - 1], dev(d, 0, o),
                )

    def rs4(l, k):
        for o in range(2):
            for d in range(1, 4):
                arrived(S2R.at[l, k, o, d - 1], x3s.at[l, k, o, d - 1], x3r.at[l, k, o, d - 1])
            total = B[l, k, o, firsts[o]].astype(F32)
            for d in range(3):
                total = total + S2R[l, k, o, d].astype(F32)
            T[pl.ds(0, 24), pl.ds(HALF * o, HALF)] = total
        T[pl.ds(24, 8), :] = jnp.zeros((8, C), F32)
        for j in range(4):
            S3S[l, j, k] = T[pl.ds(6 * j, 8), :].astype(BF)

    def rs5(l):
        for j in range(4):
            target = column + 4 * c + j

            @pl.when(target != me)
            def _():
                remote(S3S.at[l, j], S3R.at[l, z], x4s.at[l, j], x4r.at[l, z], target).start()

            @pl.when(target == me)
            def _():
                S3R[l, z] = S3S[l, j]

    def rs6(l):
        for zs in range(4):
            source = column + 2 * zs + cc

            @pl.when(source != me)
            def _():
                arrived(S3R.at[l, zs], x4s.at[l, 0], x4r.at[l, zs])

        total = S3R[l, 0].astype(F32)
        for zs in range(1, 4):
            total = total + S3R[l, zs].astype(F32)
        gout[l] = total * scale
        pltpu.make_async_copy(gout.at[l], gr_hbm.at[l], lsem.at[2 + l]).start()

    def rs_sent(l):
        for j in range(4):
            target = column + 4 * c + j

            @pl.when(target != me)
            def _():
                remote(S3S.at[l, j], S3R.at[l, z], x4s.at[l, j], x4r.at[l, z], target).wait_send()

    load_x.wait()
    tiles(act_one, 2)
    pl.semaphore_wait(barrier, len(greet))
    column_send(0)
    tiles(act_one, 4, TM, 2)
    column_wait(0)
    repack(0)
    ag_p1(0, 1)
    ag_p1(0, 0)
    ag_p1(0, 2)
    column_send(1)
    halo_send(a1p, DILATION_A, 0)
    ag_p2(0, 1)
    ag_p2(0, 0)
    ag_p2(0, 2)
    column_wait(1)
    repack(1)
    load_g.wait()
    ag_f(0, 1)
    ag_p1(1, 1)
    ag_p1(1, 0)
    ag_p1(1, 2)
    ag_f(0, 0)
    halo_send(g2p, DILATION_B, 2)
    halo_wait(a1p, DILATION_A, 0)
    ag_e(0, 1)
    ag_f(0, 2)
    ag_p2(1, 1)
    ag_done(0, 1)
    tiles(first_a, 4)
    ag_e(0, 0)
    ag_p2(1, 0)
    ag_p2(1, 2)
    ag_e(0, 2)
    ag_done(0, 0)
    tiles(first_b, 4)
    ag_done(0, 2)
    ag_f(1, 1)
    tiles(first, 2)
    ag_f(1, 0)
    ag_e(1, 1)
    tiles(first, 4, TM, 2)
    ag_f(1, 2)
    ag_e(1, 0)
    halo_send(a2p, DILATION_B, 1)
    halo_wait(g2p, DILATION_B, 2)
    weight_grad(at2, g2p, DILATION_B, 1, 1)
    weight_grad(at2, g2p, DILATION_B, 1, 2)
    ag_e(1, 2)
    rs1(1, 1)
    weight_grad(at2, g2p, DILATION_B, 1, 0)
    rs1(1, 2)
    for k in range(3):
        ag_done(1, k)
    tile(second, 0)
    rs2(1, 1)
    tile(second, 3)
    halo_send(g1p, DILATION_A, 3)
    rs1(1, 0)
    rs2(1, 2)
    tile(second, 1)
    rs3(1, 1)
    tile(second, 2)
    rs2(1, 0)
    rs3(1, 2)
    weight_grad(at1, g1p, DILATION_A, 0, 1)
    rs4(1, 1)
    halo_wait(g1p, DILATION_A, 3)
    weight_grad(at1, g1p, DILATION_A, 0, 2)
    rs1(0, 1)
    rs3(1, 0)
    weight_grad(at1, g1p, DILATION_A, 0, 0)
    rs1(0, 2)
    rs4(1, 2)
    halo_wait(a2p, DILATION_B, 1)
    halo_sent(g2p, DILATION_B, 2)
    tile(last_forward, 0)
    rs1(0, 0)
    rs2(0, 1)
    tile(last_forward, 1)
    rs2(0, 2)
    rs4(1, 0)
    rs5(1)
    tile(last_forward, 2)
    rs2(0, 0)
    rs3(0, 1)
    tile(last_forward, 3)
    store_out.start()
    rs3(0, 2)
    halo_sent(a2p, DILATION_B, 1)
    tile(last_backward, 0)
    rs3(0, 0)
    rs4(0, 1)
    tile(last_backward, 1)
    rs4(0, 2)
    tile(last_backward, 2)
    rs4(0, 0)
    rs5(0)
    tile(last_backward, 3)
    store_in.start()
    rs6(1)
    rs6(0)

    for copy in sent:
        copy.wait_send()
    halo_sent(a1p, DILATION_A, 0)
    halo_sent(g1p, DILATION_A, 3)
    for l in range(2):
        column_sent(l)
        rs_sent(l)
        pltpu.make_async_copy(gout.at[l], gr_hbm.at[l], lsem.at[2 + l]).wait()
    store_out.wait()
    store_in.wait()


def per_device(inputs, weight_one, weight_two, cotangent):
    scale = 1.0 / math.sqrt(inputs.shape[0] * lax.axis_size("seq"))
    shards = jnp.stack([weight_one, weight_two]).transpose(0, 2, 1, 3)
    shards = jnp.pad(shards, ((0, 0), (0, 0), (0, 2), (0, 0)))
    anywhere = pl.BlockSpec(memory_space=pl.ANY)
    vmem = pltpu.VMEM
    dma = pltpu.SemaphoreType.DMA

    def kernel(*refs):
        body(scale, *refs)

    outputs, input_grad, grads = pl.pallas_call(
        kernel,
        out_shape=(
            jax.ShapeDtypeStruct((L, C), BF),
            jax.ShapeDtypeStruct((L, C), BF),
            jax.ShapeDtypeStruct((2, 3, 8, C), F32),
        ),
        in_specs=[anywhere] * 3,
        out_specs=(anywhere,) * 3,
        scratch_shapes=[
            vmem((L, C), BF),
            vmem((L + 2 * DILATION_A, C), BF),
            vmem((L, C), BF),
            vmem((L + 2 * DILATION_B, C), BF),
            vmem((L + 2 * DILATION_B, C), BF),
            vmem((L + 2 * DILATION_A, C), BF),
            vmem((C, L), BF),
            vmem((C, L), BF),
            vmem((2, 3, 4, 4, 2, 24, C), BF),
            vmem((L, C), F32),
            vmem((L, C), F32),
            vmem((L, 1), F32),
            vmem((L, 1), F32),
            vmem((2, 3, 16, 2, 24, C), BF),
            vmem((2, 3, 4, 8, C), BF),
            vmem((2, 3, 16, 24, C), BF),
            vmem((2, 3, 2, 4, 4, 24, HALF), BF),
            vmem((2, 3, 2, 4, 24, HALF), BF),
            vmem((2, 3, 2, 2, 4, 24, HALF), BF),
            vmem((2, 3, 2, 4, 24, HALF), BF),
            vmem((2, 3, 2, 3, 24, HALF), BF),
            vmem((32, C), F32),
            vmem((2, 4, 3, 8, C), BF),
            vmem((2, 4, 3, 8, C), BF),
            vmem((2, 3, 8, C), F32),
            dma((6,)),
            dma((2, 4)), dma((2, 4)),
            dma((4, 2)), dma((4, 2)),
            dma((2, 3, 2, 3)), dma((2, 3, 2, 3)),
            dma((2, 3, 2, 2)), dma((2, 3, 2, 2)),
            dma((2, 3, 2, 2)), dma((2, 3, 2, 2)),
            dma((2, 3, 2, 4)), dma((2, 3, 2, 4)),
            dma((2, 3)), dma((2, 3)),
            dma((2, 3, 2, 2)), dma((2, 3, 2, 2)),
            dma((2, 3, 2, 2)), dma((2, 3, 2, 2)),
            dma((2, 3, 2, 3)), dma((2, 3, 2, 3)),
            dma((2, 4)), dma((2, 4)),
        ],
        compiler_params=pltpu.CompilerParams(
            collective_id=0, has_side_effects=True, vmem_limit_bytes=50500000
        ),
    )(inputs, cotangent, shards)
    grads = grads[:, :, :6, :].transpose(0, 2, 1, 3)
    return (outputs, input_grad, grads[0], grads[1])


def solution(mesh):
    in_specs = (P("seq", None), P("seq", None, None), P("seq", None, None), P("seq", None))
    out_specs = (P("seq", None), P("seq", None), P("seq", None, None), P("seq", None, None))
    return jax.shard_map(
        per_device, mesh=mesh, in_specs=in_specs, out_specs=out_specs, check_vma=False
    )
```

```python
import math

import jax
import jax.numpy as jnp
from jax import lax
from jax.experimental import pallas as pl
from jax.experimental.pallas import tpu as pltpu
from jax.sharding import PartitionSpec as P

DILATION_A = 32
DILATION_B = 64
N = 128
C = 768
HALF = C // 2
L = 1024
BF = jnp.bfloat16
F32 = jnp.float32
MESH = pl.DeviceIdType.MESH
TM = 256


def body(
    scale,
    x_hbm, g_hbm, w_hbm,
    out_hbm, ig_hbm, gr_hbm,
    xb, a1p, h, a2p, g2p, g1p, at1, at2, W, s1, s2, ir1, ir2, G, stage, R0, A, H1, R1, B, S2R, T, S3S, S3R, gout,
    lsem, cs, cr, hs, hr, p1s, p1r, p2s, p2r, fs, fr, bs, br,
    x0s, x0r, x1s, x1r, x2s, x2r, x3s, x3r, x4s, x4r,
):
    me = lax.axis_index("seq")
    c = lax.rem(me, 2)
    z = lax.rem(me // 2, 4)
    y = lax.rem(me // 8, 4)
    x = me // 32

    def place(df, ds, o):
        dx, dy = (df, ds) if o == 0 else (ds, df)
        return lax.rem(x + dx, 4), lax.rem(y + dy, 4)

    def dev(df, ds, o):
        xx, yy = place(df, ds, o)
        return (4 * xx + yy) * 8 + 2 * z + c

    firsts = (x, y)
    seconds = (y, x)
    sibling = me + 1 - 2 * c
    left = lax.rem(me + N - 1, N)
    right = lax.rem(me + 1, N)
    column = (4 * x + y) * 8

    def remote(src, dst, send, recv, target):
        return pltpu.make_async_remote_copy(
            src_ref=src, dst_ref=dst, send_sem=send, recv_sem=recv, device_id=(target,), device_id_type=MESH
        )

    sent = []

    def send(*args):
        copy = remote(*args)
        copy.start()
        sent.append(copy)

    def arrived(dst, send_sem, recv_sem):
        remote(dst, dst, send_sem, recv_sem, sibling).wait_recv()

    load_x = pltpu.make_async_copy(x_hbm, xb, lsem.at[0])
    load_x.start()
    load_g = pltpu.make_async_copy(g_hbm, g2p.at[pl.ds(DILATION_B, L)], lsem.at[1])
    load_g.start()

    barrier = pltpu.get_barrier_semaphore()
    greet = [column + lax.rem(me - column + k, 8) for k in range(1, 8)]
    for o in range(2):
        greet += [dev(k, 0, o) for k in range(1, 4)]
    greet += [left, right]
    for target in greet:
        pl.semaphore_signal(barrier, inc=1, device_id=(target,), device_id_type=MESH)

    cc = z // 2
    slot = 2 * lax.rem(z, 2) + c

    def column_send(l):
        for zt in range(4):
            target = column + 2 * zt + cc

            @pl.when(target != me)
            def _():
                remote(w_hbm.at[l], stage.at[l, :, slot], cs.at[l, zt], cr.at[l, slot], target).start()

            @pl.when(target == me)
            def _():
                pltpu.make_async_copy(w_hbm.at[l], stage.at[l, :, slot], cr.at[l, slot]).start()

    def column_wait(l):
        for j in range(4):
            source = column + 4 * c + j

            @pl.when(source != me)
            def _():
                arrived(stage.at[l, :, j], cs.at[l, 0], cr.at[l, j])

            @pl.when(source == me)
            def _():
                pltpu.make_async_copy(w_hbm.at[l], stage.at[l, :, j], cr.at[l, j]).wait()

    def column_sent(l):
        for zt in range(4):
            target = column + 2 * zt + cc

            @pl.when(target != me)
            def _():
                remote(w_hbm.at[l], stage.at[l, :, slot], cs.at[l, zt], cr.at[l, slot], target).wait_send()

    def repack(l):
        row = lax.broadcasted_iota(jnp.int32, (24, 32), 0)
        col = lax.broadcasted_iota(jnp.int32, (24, 32), 1)
        pick = jnp.where(col == (row // 6) * 8 + lax.rem(row, 6), 1.0, 0.0).astype(BF)
        for k in range(3):
            dense = jnp.dot(pick, stage[l, k].reshape(32, C), preferred_element_type=F32)
            W[l, k, x, y, c] = dense.astype(BF)

    OFFSET = (0, 3, 1, 2)

    def share(k, o, d):
        width = 128 if (k + o + d) % 2 == 0 else 256
        return HALF * o + (0 if d == 0 else HALF - width), width

    def grp(l, k, o, n, half, start=None, width=HALF):
        cols = pl.ds(HALF * o if start is None else start, width)
        s = lax.rem(seconds[o] + OFFSET[n], 4)
        if o == 0:
            return W.at[l, k, :, s, half, :, cols]
        return W.at[l, k, s, :, half, :, cols]

    def ag_p1(l, k):
        for o in range(2):
            for d in range(1, 4):
                ref = W.at[l, k, x, y, c, :, pl.ds(HALF * o, HALF)]
                send(ref, ref, p1s.at[l, k, o, d - 1], p1r.at[l, k, o, d - 1], dev(d, 0, o))

    def to_sibling(l, k, o, n):
        ref = grp(l, k, o, n, c)
        send(ref, ref, bs.at[l, k, o, n], br.at[l, k, o, n], sibling)

    def ag_p2(l, k):
        for o in range(2):
            for d in range(1, 4):
                xx, yy = place(4 - d, 0, o)
                arrived(W.at[l, k, xx, yy, c, :, pl.ds(HALF * o, HALF)], p1s.at[l, k, o, d - 1], p1r.at[l, k, o, d - 1])
            for d in range(2):
                ref = grp(l, k, o, 0, c)
                send(ref, ref, p2s.at[l, k, o, d], p2r.at[l, k, o, d], dev(0, 1 + 2 * d, o))
            to_sibling(l, k, o, 0)

    def ag_f(l, k):
        for o in range(2):
            for d in range(2):
                arrived(grp(l, k, o, 1 + d, c), p2s.at[l, k, o, d], p2r.at[l, k, o, d])
                part = grp(l, k, o, 1 + d, c, *share(k, o, d))
                send(part, part, fs.at[l, k, o, d], fr.at[l, k, o, d], dev(0, 1 + 2 * d, o))
                to_sibling(l, k, o, 1 + d)

    def ag_e(l, k):
        for o in range(2):
            for d in range(2):
                arrived(grp(l, k, o, 3, c, *share(k, o, d)), fs.at[l, k, o, d], fr.at[l, k, o, d])
            to_sibling(l, k, o, 3)

    def ag_done(l, k):
        for o in range(2):
            for n in range(4):
                arrived(grp(l, k, o, n, 1 - c), bs.at[l, k, o, n], br.at[l, k, o, n])

    def halo_copies(ref, d, n):
        return (
            remote(ref.at[pl.ds(L, d)], ref.at[pl.ds(0, d)], hs.at[n, 0], hr.at[n, 0], right),
            remote(ref.at[pl.ds(d, d)], ref.at[pl.ds(L + d, d)], hs.at[n, 1], hr.at[n, 1], left),
        )

    def halo_send(ref, d, n):
        for copy in halo_copies(ref, d, n):
            copy.start()

    def halo_sent(ref, d, n):
        for copy in halo_copies(ref, d, n):
            copy.wait_send()

    def halo_wait(ref, d, n):
        arrived(ref.at[pl.ds(0, d)], hs.at[n, 0], hr.at[n, 0])
        arrived(ref.at[pl.ds(L + d, d)], hs.at[n, 1], hr.at[n, 1])

        @pl.when(me == 0)
        def _():
            ref[pl.ds(0, d), :] = jnp.zeros((d, C), BF)

        @pl.when(me == N - 1)
        def _():
            ref[pl.ds(L + d, d), :] = jnp.zeros((d, C), BF)

    def activate(xf, t0, ap, d, at, s_ref, ir_ref):
        inv = lax.rsqrt(jnp.mean(xf * xf, axis=-1, keepdims=True) + 1e-06)
        normed = xf * inv
        gate = 0.5 * (1.0 + lax.erf(normed * 0.7071067811865476))
        active = (normed * gate).astype(BF)
        ap[pl.ds(pl.multiple_of(t0 + d, 32), TM), :] = active
        at[:, pl.ds(t0, TM)] = active.T
        s_ref[pl.ds(t0, TM), :] = gate + normed * jnp.exp(-0.5 * normed * normed) * 0.3989422804014327
        ir_ref[pl.ds(t0, TM), :] = inv

    def tiles(fn, count, size=TM, low=0):
        def step(i, carry):
            fn(pl.multiple_of(i * size, size))
            return carry

        lax.fori_loop(low, count, step, 0)

    def tile(fn, i):
        tiles(fn, i + 1, TM, i)

    def weight(l, k):
        return W[l, k].reshape(C, C)

    def term(ap, d, l, k, t0):
        return jnp.dot(ap[pl.ds(pl.multiple_of(t0 + k * d, 32), TM), :], weight(l, k), preferred_element_type=F32)

    def forward(ap, d, l, t0):
        acc = jnp.zeros((TM, C), F32)
        for k in range(3):
            acc = acc + term(ap, d, l, k, t0)
        return acc

    def backward(gp, d, l, x_ref, s_ref, ir_ref, t0):
        acc = jnp.zeros((TM, C), F32)
        for k in range(3):
            acc = acc + lax.dot_general(
                gp[pl.ds(pl.multiple_of(t0 + (2 - k) * d, 32), TM), :],
                weight(l, k),
                (((1,), (1,)), ((), ())),
                preferred_element_type=F32,
            )
        rows = pl.ds(t0, TM)
        inv = ir_ref[rows, :]
        normed = x_ref[rows, :].astype(F32) * inv
        norm_grad = acc * s_ref[rows, :]
        mean = jnp.mean(norm_grad * normed, axis=-1, keepdims=True)
        own = gp[pl.ds(pl.multiple_of(t0 + d, 32), TM), :].astype(F32)
        return (own + inv * (norm_grad - normed * mean)).astype(BF)

    def weight_grad(at, gp, d, l, k):
        rhs_start = (2 - k) * d

        def one(t0):
            acc = jnp.dot(at[pl.ds(t0, 384), :], gp[pl.ds(rhs_start, L), :], preferred_element_type=F32)
            G[l, k, pl.ds(t0 // 48, 8)] = acc.astype(BF).reshape(8, 2, 24, C)

        tiles(one, 2, 384)
        send(G.at[l, k, :, 1 - c], R0.at[l, k], x0s.at[l, k], x0r.at[l, k], sibling)

    def act_one(t0):
        activate(xb[pl.ds(t0, TM), :].astype(F32), t0, a1p, DILATION_A, at1, s1, ir1)

    def first_a(t0):
        s2[pl.ds(t0, TM), :] = term(a1p, DILATION_A, 0, 1, t0)

    def first_b(t0):
        s2[pl.ds(t0, TM), :] += term(a1p, DILATION_A, 0, 0, t0)

    def first(t0):
        mixed = s2[pl.ds(t0, TM), :] + term(a1p, DILATION_A, 0, 2, t0)
        out = (xb[pl.ds(t0, TM), :].astype(F32) + mixed).astype(BF)
        h[pl.ds(t0, TM), :] = out
        activate(out.astype(F32), t0, a2p, DILATION_B, at2, s2, ir2)

    def second(t0):
        passed = backward(g2p, DILATION_B, 1, h, s2, ir2, t0)
        g1p[pl.ds(pl.multiple_of(t0 + DILATION_A, 32), TM), :] = passed

    def last_forward(t0):
        mixed = forward(a2p, DILATION_B, 1, t0)
        rows = pl.ds(t0, TM)
        g2p[rows, :] = (h[rows, :].astype(F32) + mixed).astype(BF)

    def last_backward(t0):
        a2p[pl.ds(t0, TM), :] = backward(g1p, DILATION_A, 0, xb, s1, ir1, t0)

    store_out = pltpu.make_async_copy(g2p.at[pl.ds(0, L)], out_hbm, lsem.at[4])
    store_in = pltpu.make_async_copy(a2p.at[pl.ds(0, L)], ig_hbm, lsem.at[5])

    def rs1(l, k):
        arrived(R0.at[l, k], x0s.at[l, k], x0r.at[l, k])

        def add(pair, carry):
            for n in range(8):
                hi, lo = 2 * pair + n // 4, n % 4
                total = G[l, k, 4 * hi + lo, c] + R0[l, k, 4 * hi + lo]
                A[l, k, 0, lo, hi] = total[:, :HALF]
                A[l, k, 1, hi, lo] = total[:, HALF:]
            return carry

        lax.fori_loop(0, 2, add, 0)
        for o in range(2):
            far = lax.rem(seconds[o] + 2, 4)
            for d in range(2):
                start, width = share(k, o, d)
                cols = pl.ds(start - HALF * o, width)
                send(
                    A.at[l, k, o, far, :, :, cols], H1.at[l, k, o, :, :, cols],
                    x1s.at[l, k, o, d], x1r.at[l, k, o, d], dev(0, 1 + 2 * d, o),
                )

    def rs2(l, k):
        for o in range(2):
            for d in range(2):
                start, width = share(k, o, d)
                cols = pl.ds(start - HALF * o, width)
                arrived(H1.at[l, k, o, :, :, cols], x1s.at[l, k, o, d], x1r.at[l, k, o, d])
                near = lax.rem(seconds[o] + 1 + 2 * d, 4)
                A[l, k, o, near, :, :, cols] = A[l, k, o, near, :, :, cols] + H1[l, k, o, :, :, cols]
                send(
                    A.at[l, k, o, near], R1.at[l, k, o, d],
                    x2s.at[l, k, o, d], x2r.at[l, k, o, d], dev(0, 1 + 2 * d, o),
                )

    def rs3(l, k):
        for o in range(2):
            for d in range(2):
                arrived(R1.at[l, k, o, d], x2s.at[l, k, o, d], x2r.at[l, k, o, d])
            B[l, k, o] = (
                A[l, k, o, seconds[o]].astype(F32) + R1[l, k, o, 0].astype(F32) + R1[l, k, o, 1].astype(F32)
            ).astype(BF)
            for d in range(1, 4):
                send(
                    B.at[l, k, o, lax.rem(firsts[o] + d, 4)], S2R.at[l, k, o, d - 1],
                    x3s.at[l, k, o, d - 1], x3r.at[l, k, o, d - 1], dev(d, 0, o),
                )

    def rs4(l, k):
        for o in range(2):
            for d in range(1, 4):
                arrived(S2R.at[l, k, o, d - 1], x3s.at[l, k, o, d - 1], x3r.at[l, k, o, d - 1])
            total = B[l, k, o, firsts[o]].astype(F32)
            for d in range(3):
                total = total + S2R[l, k, o, d].astype(F32)
            T[pl.ds(0, 24), pl.ds(HALF * o, HALF)] = total
        T[pl.ds(24, 8), :] = jnp.zeros((8, C), F32)
        for j in range(4):
            S3S[l, j, k] = T[pl.ds(6 * j, 8), :].astype(BF)

    def rs5(l):
        for j in range(4):
            target = column + 4 * c + j

            @pl.when(target != me)
            def _():
                remote(S3S.at[l, j], S3R.at[l, z], x4s.at[l, j], x4r.at[l, z], target).start()

            @pl.when(target == me)
            def _():
                S3R[l, z] = S3S[l, j]

    def rs6(l):
        for zs in range(4):
            source = column + 2 * zs + cc

            @pl.when(source != me)
            def _():
                arrived(S3R.at[l, zs], x4s.at[l, 0], x4r.at[l, zs])

        total = S3R[l, 0].astype(F32)
        for zs in range(1, 4):
            total = total + S3R[l, zs].astype(F32)
        gout[l] = total * scale
        pltpu.make_async_copy(gout.at[l], gr_hbm.at[l], lsem.at[2 + l]).start()

    def rs_sent(l):
        for j in range(4):
            target = column + 4 * c + j

            @pl.when(target != me)
            def _():
                remote(S3S.at[l, j], S3R.at[l, z], x4s.at[l, j], x4r.at[l, z], target).wait_send()

    load_x.wait()
    tiles(act_one, 2)
    pl.semaphore_wait(barrier, len(greet))
    column_send(0)
    tiles(act_one, 4, TM, 2)
    column_wait(0)
    repack(0)
    ag_p1(0, 1)
    ag_p1(0, 0)
    ag_p1(0, 2)
    column_send(1)
    halo_send(a1p, DILATION_A, 0)
    ag_p2(0, 1)
    ag_p2(0, 0)
    ag_p2(0, 2)
    column_wait(1)
    repack(1)
    load_g.wait()
    ag_f(0, 1)
    ag_p1(1, 1)
    ag_p1(1, 0)
    ag_p1(1, 2)
    ag_f(0, 0)
    halo_send(g2p, DILATION_B, 2)
    halo_wait(a1p, DILATION_A, 0)
    ag_e(0, 1)
    ag_f(0, 2)
    ag_p2(1, 1)
    ag_done(0, 1)
    tiles(first_a, 4)
    ag_e(0, 0)
    ag_p2(1, 0)
    ag_p2(1, 2)
    ag_e(0, 2)
    ag_done(0, 0)
    tiles(first_b, 4)
    ag_done(0, 2)
    ag_f(1, 1)
    tiles(first, 2)
    ag_f(1, 0)
    ag_e(1, 1)
    tiles(first, 4, TM, 2)
    ag_f(1, 2)
    ag_e(1, 0)
    halo_send(a2p, DILATION_B, 1)
    halo_wait(g2p, DILATION_B, 2)
    weight_grad(at2, g2p, DILATION_B, 1, 1)
    weight_grad(at2, g2p, DILATION_B, 1, 2)
    ag_e(1, 2)
    rs1(1, 1)
    weight_grad(at2, g2p, DILATION_B, 1, 0)
    rs1(1, 2)
    for k in range(3):
        ag_done(1, k)
    tile(second, 0)
    rs2(1, 1)
    tile(second, 3)
    halo_send(g1p, DILATION_A, 3)
    rs1(1, 0)
    rs2(1, 2)
    tile(second, 1)
    rs3(1, 1)
    tile(second, 2)
    rs2(1, 0)
    rs3(1, 2)
    weight_grad(at1, g1p, DILATION_A, 0, 1)
    rs4(1, 1)
    halo_wait(g1p, DILATION_A, 3)
    weight_grad(at1, g1p, DILATION_A, 0, 2)
    rs1(0, 1)
    rs3(1, 0)
    weight_grad(at1, g1p, DILATION_A, 0, 0)
    rs1(0, 2)
    rs4(1, 2)
    halo_wait(a2p, DILATION_B, 1)
    halo_sent(g2p, DILATION_B, 2)
    tile(last_forward, 0)
    rs1(0, 0)
    rs2(0, 1)
    tile(last_forward, 1)
    rs2(0, 2)
    rs4(1, 0)
    rs5(1)
    tile(last_forward, 2)
    rs2(0, 0)
    rs3(0, 1)
    tile(last_forward, 3)
    store_out.start()
    rs3(0, 2)
    halo_sent(a2p, DILATION_B, 1)
    tile(last_backward, 0)
    rs3(0, 0)
    rs4(0, 1)
    tile(last_backward, 1)
    rs4(0, 2)
    tile(last_backward, 2)
    rs4(0, 0)
    rs5(0)
    tile(last_backward, 3)
    store_in.start()
    rs6(1)
    rs6(0)

    for copy in sent:
        copy.wait_send()
    halo_sent(a1p, DILATION_A, 0)
    halo_sent(g1p, DILATION_A, 3)
    for l in range(2):
        column_sent(l)
        rs_sent(l)
        pltpu.make_async_copy(gout.at[l], gr_hbm.at[l], lsem.at[2 + l]).wait()
    store_out.wait()
    store_in.wait()


def per_device(inputs, weight_one, weight_two, cotangent):
    scale = 1.0 / math.sqrt(inputs.shape[0] * lax.axis_size("seq"))
    shards = jnp.stack([weight_one, weight_two]).transpose(0, 2, 1, 3)
    shards = jnp.pad(shards, ((0, 0), (0, 0), (0, 2), (0, 0)))
    anywhere = pl.BlockSpec(memory_space=pl.ANY)
    vmem = pltpu.VMEM
    dma = pltpu.SemaphoreType.DMA

    def kernel(*refs):
        body(scale, *refs)

    outputs, input_grad, grads = pl.pallas_call(
        kernel,
        out_shape=(
            jax.ShapeDtypeStruct((L, C), BF),
            jax.ShapeDtypeStruct((L, C), BF),
            jax.ShapeDtypeStruct((2, 3, 8, C), F32),
        ),
        in_specs=[anywhere] * 3,
        out_specs=(anywhere,) * 3,
        scratch_shapes=[
            vmem((L, C), BF),
            vmem((L + 2 * DILATION_A, C), BF),
            vmem((L, C), BF),
            vmem((L + 2 * DILATION_B, C), BF),
            vmem((L + 2 * DILATION_B, C), BF),
            vmem((L + 2 * DILATION_A, C), BF),
            vmem((C, L), BF),
            vmem((C, L), BF),
            vmem((2, 3, 4, 4, 2, 24, C), BF),
            vmem((L, C), F32),
            vmem((L, C), F32),
            vmem((L, 1), F32),
            vmem((L, 1), F32),
            vmem((2, 3, 16, 2, 24, C), BF),
            vmem((2, 3, 4, 8, C), BF),
            vmem((2, 3, 16, 24, C), BF),
            vmem((2, 3, 2, 4, 4, 24, HALF), BF),
            vmem((2, 3, 2, 4, 24, HALF), BF),
            vmem((2, 3, 2, 2, 4, 24, HALF), BF),
            vmem((2, 3, 2, 4, 24, HALF), BF),
            vmem((2, 3, 2, 3, 24, HALF), BF),
            vmem((32, C), F32),
            vmem((2, 4, 3, 8, C), BF),
            vmem((2, 4, 3, 8, C), BF),
            vmem((2, 3, 8, C), F32),
            dma((6,)),
            dma((2, 4)), dma((2, 4)),
            dma((4, 2)), dma((4, 2)),
            dma((2, 3, 2, 3)), dma((2, 3, 2, 3)),
            dma((2, 3, 2, 2)), dma((2, 3, 2, 2)),
            dma((2, 3, 2, 2)), dma((2, 3, 2, 2)),
            dma((2, 3, 2, 4)), dma((2, 3, 2, 4)),
            dma((2, 3)), dma((2, 3)),
            dma((2, 3, 2, 2)), dma((2, 3, 2, 2)),
            dma((2, 3, 2, 2)), dma((2, 3, 2, 2)),
            dma((2, 3, 2, 3)), dma((2, 3, 2, 3)),
            dma((2, 4)), dma((2, 4)),
        ],
        compiler_params=pltpu.CompilerParams(
            collective_id=0, has_side_effects=True, vmem_limit_bytes=50500000
        ),
    )(inputs, cotangent, shards)
    grads = grads[:, :, :6, :].transpose(0, 2, 1, 3)
    return (outputs, input_grad, grads[0], grads[1])


def solution(mesh):
    in_specs = (P("seq", None), P("seq", None, None), P("seq", None, None), P("seq", None))
    out_specs = (P("seq", None), P("seq", None), P("seq", None, None), P("seq", None, None))
    return jax.shard_map(
        per_device, mesh=mesh, in_specs=in_specs, out_specs=out_specs, check_vma=False
    )
```
